512 devices in a mesh: view: 8 (over z_hi, x), col: 64 (over y, z_lo, core).
Axes of the slice: x: 4, y: 8, z: 8 (z_hi: 2, z_lo: 4; z = z_hi * 4 + z_lo), core: 2. Of those that a mesh axis runs over, the one named last changes fastest.
Arguments:
- estimate: float32 [2048, 64, 128], P('col', 'view'), may hold values from 0.5 to 2
- observed: float32 [8, 2048, 64, 128], P('view', 'col'), may hold values from 0.5 to 2
- psf_taps: float32 [8, 3, 31], replicated, as said below
- intersection: int32 [8, 16], replicated, may hold values 0 or 1
Outputs:
- deconvolved: float32 [2048, 64, 128], P('col', 'view')
The draws below stay inside these ranges and needn't reach their ends.
Inputs may be any that keep to these rules, and one draw needn't show every extreme that they name: `psf_taps`: every tap is positive.
All inputs are finite; a program needn't handle non-finite values.
Results may differ from the reference program's by a relative error of at most 0.0003.
Values sent between devices are 32-bit elements; how exact they have to be, the bound alone decides.
No kernel may reach another device: no remote copies, remote signals or barrier semaphores. Data moves between devices by JAX's collectives and lax.ppermute only.
A program may use at most 64 MiB of HBM per device.

```python
import math
from functools import partial
import jax
import jax.numpy as jnp
from jax import lax

TX = 128
NY = 64
NZ = 128
TAPS = 31
ITERS = 2
VIEWS = 8
NX = 2048
TILES = 16


def draw_psf_taps(key, part):
    key_order = jax.random.fold_in(key, 10)
    key_width = jax.random.fold_in(key, 11)
    key_rough = jax.random.fold_in(key, 12)
    key_axis = jax.random.fold_in(key, 13)
    order = jax.random.permutation(key_order, VIEWS).astype(jnp.float32)
    spread = jax.random.uniform(key_width, (VIEWS,), jnp.float32, 0.0, 1.0)
    position = (order + spread) / VIEWS
    base = 0.4 * jnp.exp(position * jnp.log(40.0))
    axis_factor = jnp.exp(jax.random.uniform(key_axis, (VIEWS, 3, 1), jnp.float32, -0.15, 0.15))
    widths = base[:, None, None] * axis_factor
    offsets = jnp.arange(TAPS, dtype=jnp.float32) - (TAPS - 1) // 2
    envelope = jnp.exp(-0.5 * (offsets[None, None, :] / widths) ** 2) + 0.001
    rough = jnp.exp(jax.random.uniform(key_rough, (VIEWS, 3, TAPS), jnp.float32, -0.4, 0.4))
    return (envelope * rough).astype(jnp.float32)


def touch_ends(drawn, stream_key, low, top_value):
    longest = drawn.shape.index(max(drawn.shape))
    spots = []
    for shift in (0, 1):
        where = [jax.random.randint(jax.random.fold_in(stream_key, axis), (), 0, length) for axis, length in enumerate(drawn.shape)]
        where[longest] = (where[longest] + shift) % drawn.shape[longest]
        spots.append(tuple(where))
    return drawn.at[spots[0]].set(low).at[spots[1]].set(top_value)


def shard_levels(key, extent, cuts, low, largest):
    level = 1.0
    for dim, shards_of in cuts:
        heights = jax.random.uniform(jax.random.fold_in(jax.random.fold_in(key, 6), dim), (shards_of,), jnp.float32, low / len(cuts), largest / len(cuts))
        level = level * jnp.repeat(jnp.exp(heights), extent[dim] // shards_of).reshape((-1,) + (1,) * (len(extent) - 1 - dim))
    return level


def setup_inputs(seed: int = 0) -> dict:
    keys = jax.random.split(jax.random.key(seed), 5)
    return {
        "estimate": jnp.clip(jnp.exp(math.log(2.0) - 1.3862944 * jax.random.uniform(keys[0], (NX, NY, NZ), jnp.float32) ** shard_levels(keys[0], (NX, NY, NZ), ((0, 64), (1, 8)), -0.2, 0.2)), 0.5, 2.0),
        "observed": jnp.clip(jnp.exp(math.log(2.0) - 1.3862944 * jax.random.uniform(keys[1], (VIEWS, NX, NY, NZ), jnp.float32) ** shard_levels(keys[1], (VIEWS, NX, NY, NZ), ((0, 8), (1, 64)), -0.2, 0.2)), 0.5, 2.0),
        "psf_taps": draw_psf_taps(jax.random.fold_in(keys[4], 71), 0),
        "intersection": touch_ends((jax.random.randint(keys[3], (VIEWS, TILES), 0, 3) < 2).astype(jnp.int32), jax.random.fold_in(keys[3], 1), 0, 1),
    }


HIGH = lax.Precision.HIGHEST


def banded(kernel, length):
    tap_count = kernel.shape[0]
    half_width = (tap_count - 1) // 2
    offsets = jnp.arange(length)[:, None] - jnp.arange(length)[None, :] + half_width
    onehot = (offsets[:, :, None] == jnp.arange(tap_count)[None, None, :]).astype(kernel.dtype)
    return jnp.einsum("iok,k->io", onehot, kernel, precision=HIGH)


def column_weights(kernel, length):
    return jnp.sum(banded(kernel, length), axis=0)


def along_rows(field, kernel):
    tap_count = kernel.shape[0]
    half_width = (tap_count - 1) // 2
    row_count = field.shape[0]
    padded = jnp.pad(field, ((half_width, half_width),) + ((0, 0),) * (field.ndim - 1))
    result = kernel[0] * padded[0:row_count]
    for offset in range(1, tap_count):
        result = result + kernel[offset] * padded[offset:offset + row_count]
    return result


def across(field, kernels):
    result = jnp.einsum("xyz,yw->xwz", field, banded(kernels[1], field.shape[1]), precision=HIGH)
    return jnp.dot(result, banded(kernels[2], field.shape[2]), precision=HIGH)


def blur(field, kernels):
    return across(along_rows(field, kernels[0]), kernels)


def view_term(current, observed_view, kernel_view, mirror_view, mask_view):
    blurred = blur(current, kernel_view)
    inside = mask_view[:, None, None] > 0
    ratio = jnp.where(inside, observed_view / jnp.where(inside, blurred, 1.0), 0.0)
    return blur(ratio, mirror_view)


def accumulate(carry, items):
    current, total = carry
    observed_view, kernel_view, mirror_view, mask_view = items
    return (current, total + view_term(current, observed_view, kernel_view, mirror_view, mask_view)), None


def reference(estimate, observed, psf_taps, intersection):
    kernels = psf_taps / jnp.sum(psf_taps, axis=2, keepdims=True)
    mirrored = kernels[:, :, ::-1]
    tile_index = (jnp.arange(NX) // TX).astype(jnp.int32)
    masks = intersection[:, tile_index].astype(estimate.dtype)
    weight_rows = jax.vmap(along_rows)(masks, mirrored[:, 0])
    weight_cols = jax.vmap(partial(column_weights, length=NY))(mirrored[:, 1])
    weight_depth = jax.vmap(partial(column_weights, length=NZ))(mirrored[:, 2])
    weights = jnp.einsum("vx,vy,vz->xyz", weight_rows, weight_cols, weight_depth, precision=HIGH)
    current = estimate
    for iteration in range(ITERS):
        start = (current, jnp.zeros_like(current))
        (current, total), _ = lax.scan(accumulate, start, (observed, kernels, mirrored, masks))
        current = current * (total + 1.0) / (weights + 1.0)
    return current
```

```python
import jax
import jax.numpy as jnp
from jax import lax
from jax.sharding import PartitionSpec as P

TX = 128
ITERS = 2
HIGH = lax.Precision.HIGH
HIGHEST = lax.Precision.HIGHEST
AXES = ("view", "col")
SLAB = 16
COLS = 64


def device(h, x, c):
    return (h * 4 + x) * COLS + c


def chip_x(column, p):
    return (p - column % 4) % 4


def spread_pairs(turn):
    pairs = []
    for h in range(2):
        for column in range(COLS // 2):
            for x in range(4):
                for k in range(2):
                    p = 2 * k + (x + turn) % 2
                    pairs.append(
                        (device(h, x, 2 * column + k), device(h, chip_x(column, p), 2 * column + x // 2))
                    )
    return pairs


def chip_pairs(step):
    pairs = []
    chips = COLS // 2 * 4
    for h in range(2):
        for chip in range(chips):
            if 0 <= chip + step < chips:
                for core in range(2):
                    ends = []
                    for q in (chip, chip + step):
                        column, p = divmod(q, 4)
                        ends.append(device(h, chip_x(column, p), 2 * column + core))
                    pairs.append(tuple(ends))
    return pairs


def swap_pairs(across):
    pairs = []
    for h in range(2):
        for x in range(4):
            for c in range(COLS):
                other = device(1 - h, x, c) if across == "h" else device(h, x, c ^ 1)
                pairs.append((device(h, x, c), other))
    return pairs


def reverse(pairs):
    return [(b, a) for a, b in pairs]


SPREAD = [spread_pairs(0), spread_pairs(1)]
UP = chip_pairs(1)
DOWN = chip_pairs(-1)
SWAP_H = swap_pairs("h")
SWAP_CORE = swap_pairs("core")


def send(value, pairs):
    return lax.ppermute(value, AXES, pairs)


def tap_matrix(kernel, taps):
    count = kernel.shape[1]
    onehot = (taps[:, :, None] == jnp.arange(count, dtype=jnp.int32)).astype(jnp.float32)
    return jnp.einsum("ijk,uk->uij", onehot, kernel, precision=HIGHEST)


def body(estimate, observed, psf_taps, intersection):
    rows = intersection.shape[1] * TX
    full_width = observed.shape[2]
    depth = observed.shape[3]
    view_index = lax.axis_index("view")
    col_index = lax.axis_index("col")
    h, x = view_index // 4, view_index % 4
    column, k = col_index // 2, col_index % 2
    p = (x + column % 4) % 4
    core = k
    first_row = column * (4 * SLAB) + p * SLAB
    taps = psf_taps.shape[2]
    half = (taps - 1) // 2

    def spread(block, turn):
        return send(lax.dynamic_slice_in_dim(block, SLAB * ((x + turn) % 2), SLAB, 0), SPREAD[turn])

    even = p % 2 == 0
    est = [spread(estimate, turn) for turn in (0, 1)]
    quarter = jnp.where(even, jnp.concatenate(est, 1), jnp.concatenate(est[::-1], 1))
    current = jnp.concatenate([quarter, send(quarter, SWAP_H)], 1)
    images = jnp.stack([spread(observed[0], turn) for turn in (0, 1)])

    kernels = psf_taps / jnp.sum(psf_taps, axis=2, keepdims=True)
    views = jnp.arange(kernels.shape[0], dtype=jnp.int32)
    own_views = 4 * h + 2 * core + jnp.stack([p % 2, (p + 1) % 2])
    picker = (own_views[:, None] == views[None, :]).astype(jnp.float32)
    own = jnp.einsum("uv,vdk->udk", picker, kernels, precision=HIGHEST)
    quarters = jnp.stack([2 * h + core, 2 * (1 - h) + core, 2 * h + 1 - core, 2 * (1 - h) + 1 - core])
    quarter_width = full_width // 4
    local_y = (quarters[:, None] * quarter_width + jnp.arange(quarter_width, dtype=jnp.int32)[None, :]).reshape(-1)
    all_y = jnp.arange(full_width, dtype=jnp.int32)
    all_z = jnp.arange(depth, dtype=jnp.int32)
    slab = jnp.arange(SLAB, dtype=jnp.int32)
    wide = jnp.arange(3 * SLAB, dtype=jnp.int32) - SLAB
    mat_x = tap_matrix(own[:, 0], wide[None, :] - slab[:, None] + half)
    mat_y = tap_matrix(own[:, 1], local_y[None, :] - all_y[:, None] + half)
    mat_z = tap_matrix(own[:, 2], all_z[:, None] - all_z[None, :] + half)

    wide_rows = first_row + wide
    tile = (wide_rows // TX)[:, None] == jnp.arange(intersection.shape[1], dtype=jnp.int32)[None, :]
    tile = jnp.logical_and(tile, jnp.logical_and(wide_rows >= 0, wide_rows < rows)[:, None]).astype(jnp.float32)
    masks = jnp.einsum("vt,jt->vj", intersection.astype(jnp.float32), tile, precision=HIGHEST)
    weight_rows = jnp.einsum(
        "vrj,vj->vr", tap_matrix(kernels[:, 0], slab[:, None] - wide[None, :] + half), masks, precision=HIGHEST
    )

    def coverage(kernel, places, length):
        source = places[:, None] - jnp.arange(taps, dtype=jnp.int32)[None, :] + half
        inside = jnp.logical_and(source >= 0, source < length).astype(jnp.float32)
        return jnp.einsum("yk,vk->vy", inside, kernel, precision=HIGHEST)

    weight_cols = coverage(kernels[:, 1], local_y[: 2 * quarter_width], full_width)
    weight_depth = coverage(kernels[:, 2], all_z, depth)
    weight_plane = weight_rows[:, :, None] * weight_cols[:, None, :]
    weights = jnp.einsum("vxy,vz->xyz", weight_plane, weight_depth, precision=HIGHEST)
    own_masks = jnp.einsum("uv,vj->uj", picker, masks[:, SLAB : 2 * SLAB], precision=HIGHEST)
    inside = own_masks[:, :, None, None] > 0

    width = 2 * quarter_width
    for iteration in range(ITERS):
        low = send(current, UP)
        high = send(current, DOWN)
        extended = jnp.concatenate([low, current, high], 0)
        extended = jnp.concatenate([extended, send(extended, SWAP_CORE)], 1)
        blurred = jnp.einsum("urj,jyz->uryz", mat_x, extended, precision=HIGH)
        blurred = jnp.einsum("urjz,uyj->uryz", blurred, mat_y, precision=HIGH)
        blurred = jnp.einsum("uryz,uzw->uryw", blurred, mat_z, precision=HIGH)
        ratio = jnp.where(inside, images / jnp.where(inside, blurred, 1.0), 0.0)
        back = jnp.einsum("uryw,uzw->uryz", ratio, mat_z, precision=HIGH)
        back = jnp.einsum("uryz,uyj->urjz", back, mat_y, precision=HIGH)
        back = jnp.einsum("urj,uryz->jyz", mat_x, back, precision=HIGH)
        part = back[:, :width] + send(back[:, width:], SWAP_CORE)
        part = (
            part[SLAB : 2 * SLAB]
            + send(part[:SLAB], DOWN)
            + send(part[2 * SLAB :], UP)
        )
        if iteration < ITERS - 1:
            other = send(part, SWAP_H)
            total = part + jnp.concatenate([other[:, quarter_width:], other[:, :quarter_width]], 1)
            current = current * (total + 1.0) / (weights + 1.0)
        else:
            total = part[:, :quarter_width] + send(part[:, quarter_width:], SWAP_H)
            quarter = current[:, :quarter_width] * (total + 1.0) / (weights[:, :quarter_width] + 1.0)

    block = quarter_width // 2
    first, second = quarter[:, :block], quarter[:, block:]
    pieces = []
    for turn in (0, 1):
        chosen = jnp.where((p + turn) % 2 == 0, first, second)
        pieces.append(send(chosen, reverse(SPREAD[turn])))
    return jnp.where(x % 2 == 0, jnp.concatenate(pieces, 0), jnp.concatenate(pieces[::-1], 0))


def solution(mesh):
    return jax.shard_map(
        body,
        mesh=mesh,
        in_specs=(P("col", "view", None), P("view", "col", None, None), P(), P()),
        out_specs=P("col", "view", None),
        check_vma=False,
    )
```

```python
import jax
import jax.numpy as jnp
from jax import lax
from jax.sharding import PartitionSpec as P

TX = 128
ITERS = 2
HIGH = lax.Precision.HIGH
HIGHEST = lax.Precision.HIGHEST
AXES = ("view", "col")
SLAB = 16
COLS = 64


def device(h, x, c):
    return (h * 4 + x) * COLS + c


def chip_x(column, p):
    return (p - column % 4) % 4


def spread_pairs(turn, cross=0):
    pairs = []
    for h in range(2):
        for column in range(COLS // 2):
            for x in range(4):
                for k in range(2):
                    p = 2 * k + (x + turn) % 2
                    pairs.append(
                        (
                            device(h, x, 2 * column + k),
                            device(h ^ cross, chip_x(column, p), 2 * column + x // 2),
                        )
                    )
    return pairs


def chip_pairs(first):
    pairs = []
    for h in range(2):
        for chip in range(first, COLS // 2 * 4 - 1, 2):
            for core in range(2):
                low, high = (
                    device(h, chip_x(q // 4, q % 4), 2 * (q // 4) + core) for q in (chip, chip + 1)
                )
                pairs += [(low, high), (high, low)]
    return pairs


def swap_pairs(across):
    pairs = []
    for h in range(2):
        for x in range(4):
            for c in range(COLS):
                other = device(1 - h, x, c) if across == "h" else device(h, x, c ^ 1)
                pairs.append((device(h, x, c), other))
    return pairs


def reverse(pairs):
    return [(b, a) for a, b in pairs]


SPREAD = [spread_pairs(0), spread_pairs(1)]
SPREAD_CROSS = [spread_pairs(0, 1), spread_pairs(1, 1)]
ODD = chip_pairs(1)
EVEN = chip_pairs(0)
SWAP_H = swap_pairs("h")
SWAP_CORE = swap_pairs("core")


def send(value, pairs):
    return lax.ppermute(value, AXES, pairs)


def tap_matrix(kernel, taps):
    count = kernel.shape[1]
    onehot = (taps[:, :, None] == jnp.arange(count, dtype=jnp.int32)).astype(jnp.float32)
    return jnp.einsum("ijk,uk->uij", onehot, kernel, precision=HIGHEST)


def body(estimate, observed, psf_taps, intersection):
    rows = intersection.shape[1] * TX
    full_width = observed.shape[2]
    depth = observed.shape[3]
    view_index = lax.axis_index("view")
    col_index = lax.axis_index("col")
    h, x = view_index // 4, view_index % 4
    column, k = col_index // 2, col_index % 2
    p = (x + column % 4) % 4
    core = k
    first_row = column * (4 * SLAB) + p * SLAB
    taps = psf_taps.shape[2]
    half = (taps - 1) // 2

    def piece(block, turn):
        return lax.dynamic_slice_in_dim(block, SLAB * ((x + turn) % 2), SLAB, 0)

    even = p % 2 == 0
    est = [send(piece(estimate, turn), SPREAD[turn]) for turn in (0, 1)]
    quarter = jnp.where(even, jnp.concatenate(est, 1), jnp.concatenate(est[::-1], 1))
    current = jnp.concatenate([quarter, send(quarter, SWAP_H)], 1)
    images = [piece(observed[0], turn) for turn in (0, 1)]
    *images, _ = lax.optimization_barrier((*images, quarter))
    images = [send(image, route) for image, route in zip(images, SPREAD)]
    current, images[0] = lax.optimization_barrier((current, images[0]))

    kernels = psf_taps / jnp.sum(psf_taps, axis=2, keepdims=True)
    views = jnp.arange(kernels.shape[0], dtype=jnp.int32)
    own_views = 4 * h + 2 * core + jnp.stack([p % 2, (p + 1) % 2])
    picker = (own_views[:, None] == views[None, :]).astype(jnp.float32)
    own = jnp.einsum("uv,vdk->udk", picker, kernels, precision=HIGHEST)
    quarters = jnp.stack([2 * h + core, 2 * (1 - h) + core, 2 * h + 1 - core, 2 * (1 - h) + 1 - core])
    quarter_width = full_width // 4
    local_y = (quarters[:, None] * quarter_width + jnp.arange(quarter_width, dtype=jnp.int32)[None, :]).reshape(-1)
    all_y = jnp.arange(full_width, dtype=jnp.int32)
    all_z = jnp.arange(depth, dtype=jnp.int32)
    slab = jnp.arange(SLAB, dtype=jnp.int32)
    side = jnp.where(even, SLAB, -SLAB)
    wide = jnp.concatenate([slab - side, slab, slab + side])
    mat_x = tap_matrix(own[:, 0], wide[None, :] - slab[:, None] + half)
    mat_y = tap_matrix(own[:, 1], local_y[None, :] - all_y[:, None] + half)
    mat_z = tap_matrix(own[:, 2], all_z[:, None] - all_z[None, :] + half)

    wide_rows = first_row + wide
    tile = (wide_rows // TX)[:, None] == jnp.arange(intersection.shape[1], dtype=jnp.int32)[None, :]
    tile = jnp.logical_and(tile, jnp.logical_and(wide_rows >= 0, wide_rows < rows)[:, None]).astype(jnp.float32)
    masks = jnp.einsum("vt,jt->vj", intersection.astype(jnp.float32), tile, precision=HIGHEST)
    weight_rows = jnp.einsum(
        "vrj,vj->vr", tap_matrix(kernels[:, 0], slab[:, None] - wide[None, :] + half), masks, precision=HIGHEST
    )

    def coverage(kernel, places, length):
        source = places[:, None] - jnp.arange(taps, dtype=jnp.int32)[None, :] + half
        inside = jnp.logical_and(source >= 0, source < length).astype(jnp.float32)
        return jnp.einsum("yk,vk->vy", inside, kernel, precision=HIGHEST)

    weight_cols = coverage(kernels[:, 1], local_y[: 2 * quarter_width], full_width)
    weight_depth = coverage(kernels[:, 2], all_z, depth)
    weight_plane = weight_rows[:, :, None] * weight_cols[:, None, :]
    weights = jnp.einsum("vxy,vz->xyz", weight_plane, weight_depth, precision=HIGHEST)
    own_masks = jnp.einsum("uv,vj->uj", picker, masks[:, SLAB : 2 * SLAB], precision=HIGHEST)
    inside = own_masks[:, :, None, None] > 0

    width = 2 * quarter_width
    scale = 1.0 / (weights + 1.0)
    for iteration in range(ITERS):
        extended = jnp.concatenate([send(current, ODD), current, send(current, EVEN)], 0)
        if iteration == 0:
            extended, images[1] = lax.optimization_barrier((extended, images[1]))
            images = jnp.stack(images)
        extended = jnp.concatenate([extended, send(extended, SWAP_CORE)], 1)
        blurred = jnp.einsum("urj,jyz->uryz", mat_x, extended, precision=HIGH)
        blurred = jnp.einsum("urjz,uyj->uryz", blurred, mat_y, precision=HIGH)
        blurred = jnp.einsum("uryz,uzw->uryw", blurred, mat_z, precision=HIGH)
        ratio = jnp.where(inside, images / jnp.where(inside, blurred, 1.0), 0.0)
        back = jnp.einsum("uryw,uzw->uryz", ratio, mat_z, precision=HIGH)
        back = jnp.einsum("uryz,uyj->urjz", back, mat_y, precision=HIGH)
        back = jnp.einsum("urj,uryz->jyz", mat_x, back, precision=HIGH)
        part = back[:, :width] + send(back[:, width:], SWAP_CORE)
        part = part[SLAB : 2 * SLAB] + send(part[:SLAB], ODD) + send(part[2 * SLAB :], EVEN)
        if iteration < ITERS - 1:
            other = send(part, SWAP_H)
            total = part + jnp.concatenate([other[:, quarter_width:], other[:, :quarter_width]], 1)
            current = current * (total + 1.0) * scale

    factor = current * scale
    halves = [
        (factor * part)[:, quarter_width:],
        (factor * (part + 1.0))[:, :quarter_width],
    ]
    block = quarter_width // 2
    pieces = []
    for half_part, routes in zip(halves, (SPREAD_CROSS, SPREAD)):
        first, second = half_part[:, :block], half_part[:, block:]
        pieces.append(
            [
                send(jnp.where((p + turn) % 2 == 0, first, second), reverse(routes[turn]))
                for turn in (0, 1)
            ]
        )
    one, two = (pieces[0][turn] + pieces[1][turn] for turn in (0, 1))
    return jnp.where(x % 2 == 0, jnp.concatenate([one, two], 0), jnp.concatenate([two, one], 0))


def solution(mesh):
    return jax.shard_map(
        body,
        mesh=mesh,
        in_specs=(P("col", "view", None), P("view", "col", None, None), P(), P()),
        out_specs=P("col", "view", None),
        check_vma=False,
    )
```

```python
import jax
import jax.numpy as jnp
from jax import lax
from jax.sharding import PartitionSpec as P

TX = 128
ITERS = 2
HIGH = lax.Precision.HIGH
HIGHEST = lax.Precision.HIGHEST
AXES = ("view", "col")
SLAB = 8
COLS = 64
SLABS = 256


def device(h, x, c):
    return (h * 4 + x) * COLS + c


def holder(h, d):
    column, rest = divmod(d, 8)
    p, core = divmod(rest, 2)
    return device(h, (p - column) % 4, 2 * column + core)


def spread_pairs(turn):
    return [
        (device(h, x, 2 * column + k), holder(h, 8 * column + 4 * k + (x + turn) % 4))
        for h in range(2)
        for column in range(COLS // 2)
        for x in range(4)
        for k in range(2)
    ]


def slab_swaps(step, members):
    pairs = []
    for h in range(2):
        for d in range(SLABS - step):
            if d % 4 in members:
                low, high = holder(h, d), holder(h, d + step)
                pairs += [(low, high), (high, low)]
    return pairs


SPREAD = [spread_pairs(turn) for turn in range(4)]
RETURN = [[(b, a) for a, b in pairs] for pairs in SPREAD]
SWAP_H = [(device(h, x, c), device(1 - h, x, c)) for h in range(2) for x in range(4) for c in range(COLS)]
NEAR = [slab_swaps(2, (2, 3)), slab_swaps(1, (1, 3)), slab_swaps(2, (0, 1)), slab_swaps(1, (0, 2))]


def send(value, pairs):
    return lax.ppermute(value, AXES, pairs)


def tap_matrix(kernel, taps):
    count = kernel.shape[1]
    onehot = (taps[:, :, None] == jnp.arange(count, dtype=jnp.int32)).astype(jnp.float32)
    return jnp.einsum("ijk,uk->uij", onehot, kernel, precision=HIGHEST)


def body(estimate, observed, psf_taps, intersection):
    rows = intersection.shape[1] * TX
    full_width = observed.shape[2]
    depth = observed.shape[3]
    block = estimate.shape[1]
    view_index = lax.axis_index("view")
    col_index = lax.axis_index("col")
    h, x = view_index // 4, view_index % 4
    column, core = col_index // 2, col_index % 2
    p = (x + column) % 4
    j = 2 * (p % 2) + core
    first_row = column * (8 * SLAB) + p * (2 * SLAB) + core * SLAB
    taps = psf_taps.shape[2]
    half = (taps - 1) // 2

    def piece(value, turn):
        return lax.dynamic_slice_in_dim(value, SLAB * ((x + turn) % 4), SLAB, 0)

    other = send(estimate, SWAP_H)
    paired = jnp.where(h == 0, jnp.concatenate([estimate, other], 1), jnp.concatenate([other, estimate], 1))
    est = [send(piece(paired, turn), SPREAD[turn]) for turn in range(4)]
    current = jnp.concatenate(est[::-1] + est[:0:-1], 1)
    current = lax.dynamic_slice_in_dim(current, 2 * block * ((3 - j) % 4), full_width, 1)
    images = [send(piece(observed[0], turn), SPREAD[turn]) for turn in range(4)]

    kernels = psf_taps / jnp.sum(psf_taps, axis=2, keepdims=True)
    views = jnp.arange(kernels.shape[0], dtype=jnp.int32)
    own_views = 4 * h + (j - jnp.arange(4, dtype=jnp.int32)) % 4
    picker = (own_views[:, None] == views[None, :]).astype(jnp.float32)
    own = jnp.einsum("uv,vdk->udk", picker, kernels, precision=HIGHEST)
    all_y = jnp.arange(full_width, dtype=jnp.int32)
    local_y = all_y // (2 * block) * block + all_y % (2 * block) // block * (full_width // 2) + all_y % block
    all_z = jnp.arange(depth, dtype=jnp.int32)
    slab = jnp.arange(SLAB, dtype=jnp.int32)
    two = jnp.where(p % 2 == 0, 2 * SLAB, -2 * SLAB)
    one = jnp.where(core == 0, SLAB, -SLAB)
    wide = jnp.concatenate([slab - two, slab - one, slab + two, slab + one, slab])
    mat_x = tap_matrix(own[:, 0], wide[None, :] - slab[:, None] + half)
    mat_y = tap_matrix(own[:, 1], local_y[None, :] - all_y[:, None] + half)
    mat_z = tap_matrix(own[:, 2], all_z[:, None] - all_z[None, :] + half)

    wide_rows = first_row + wide
    tile = (wide_rows // TX)[:, None] == jnp.arange(intersection.shape[1], dtype=jnp.int32)[None, :]
    tile = jnp.logical_and(tile, jnp.logical_and(wide_rows >= 0, wide_rows < rows)[:, None]).astype(jnp.float32)
    masks = jnp.einsum("vt,jt->vj", intersection.astype(jnp.float32), tile, precision=HIGHEST)
    weight_rows = jnp.einsum(
        "vrj,vj->vr", tap_matrix(kernels[:, 0], slab[:, None] - wide[None, :] + half), masks, precision=HIGHEST
    )

    def coverage(kernel, places, length):
        source = places[:, None] - jnp.arange(taps, dtype=jnp.int32)[None, :] + half
        inside = jnp.logical_and(source >= 0, source < length).astype(jnp.float32)
        return jnp.einsum("yk,vk->vy", inside, kernel, precision=HIGHEST)

    weight_cols = coverage(kernels[:, 1], local_y, full_width)
    weight_depth = coverage(kernels[:, 2], all_z, depth)
    weight_plane = weight_rows[:, :, None] * weight_cols[:, None, :]
    weights = jnp.einsum("vxy,vz->xyz", weight_plane, weight_depth, precision=HIGHEST)
    scale = 1.0 / (weights + 1.0)
    own_masks = jnp.einsum("uv,vj->uj", picker, masks[:, 4 * SLAB :], precision=HIGHEST)
    inside = own_masks[:, :, None, None] > 0

    def own_half(value, mine):
        blocks = value.reshape(SLAB, 4, 2, block, depth)
        return jnp.where((h == 0) == mine, blocks[:, :, 0], blocks[:, :, 1])

    for iteration in range(ITERS):
        extended = jnp.concatenate([send(current, pairs) for pairs in NEAR] + [current], 0)
        if iteration == 0:
            *images, extended = lax.optimization_barrier((*images, extended))
            images = jnp.stack(images)
        blurred = jnp.einsum("urj,jyz->uryz", mat_x, extended, precision=HIGH)
        blurred = jnp.einsum("urjz,uyj->uryz", blurred, mat_y, precision=HIGH)
        blurred = jnp.einsum("uryz,uzw->uryw", blurred, mat_z, precision=HIGH)
        ratio = jnp.where(inside, images / jnp.where(inside, blurred, 1.0), 0.0)
        back = jnp.einsum("uryw,uzw->uryz", ratio, mat_z, precision=HIGH)
        back = jnp.einsum("uryz,uyj->urjz", back, mat_y, precision=HIGH)
        back = jnp.einsum("urj,uryz->jyz", mat_x, back, precision=HIGH)
        part = back[4 * SLAB :]
        for place, pairs in enumerate(NEAR):
            part = part + send(back[place * SLAB : (place + 1) * SLAB], pairs)
        if iteration < ITERS - 1:
            current = current * (part + send(part, SWAP_H) + 1.0) * scale
        else:
            total = own_half(part, True) + send(own_half(part, False), SWAP_H)
            result = own_half(current, True) * (total + 1.0) * own_half(scale, True)

    pieces = [
        send(lax.dynamic_index_in_dim(result, (j - turn) % 4, 1, keepdims=False), RETURN[turn])
        for turn in range(4)
    ]
    joined = jnp.concatenate(pieces + pieces[:3], 0)
    return lax.dynamic_slice_in_dim(joined, SLAB * ((4 - x) % 4), 4 * SLAB, 0)


def solution(mesh):
    return jax.shard_map(
        body,
        mesh=mesh,
        in_specs=(P("col", "view", None), P("view", "col", None, None), P(), P()),
        out_specs=P("col", "view", None),
        check_vma=False,
    )
```

```python
import jax
import jax.numpy as jnp
from jax import lax
from jax.sharding import PartitionSpec as P

TX = 128
ITERS = 2
HIGH = lax.Precision.HIGH
HIGHEST = lax.Precision.HIGHEST
AXES = ("view", "col")
SLAB = 16
COLS = 64


def device(h, x, c):
    return (h * 4 + x) * COLS + c


def chip_x(column, p):
    return (p - column % 4) % 4


def spread_pairs(turn):
    pairs = []
    for h in range(2):
        for column in range(COLS // 2):
            for x in range(4):
                for k in range(2):
                    p = 2 * k + (x + turn) % 2
                    pairs.append(
                        (
                            device(h, x, 2 * column + k),
                            device(h, chip_x(column, p), 2 * column + x // 2),
                        )
                    )
    return pairs


def chip_pairs(first):
    pairs = []
    for h in range(2):
        for chip in range(first, COLS // 2 * 4 - 1, 2):
            for core in range(2):
                low, high = (
                    device((h + q // 16) % 2, chip_x(q // 4, q % 4), 2 * (q // 4) + core)
                    for q in (chip, chip + 1)
                )
                pairs += [(low, high), (high, low)]
    return pairs


def swap_pairs(across):
    pairs = []
    for h in range(2):
        for x in range(4):
            for c in range(COLS):
                other = device(1 - h, x, c) if across == "h" else device(h, x, c ^ 1)
                pairs.append((device(h, x, c), other))
    return pairs


def reverse(pairs):
    return [(b, a) for a, b in pairs]


SPREAD = [spread_pairs(0), spread_pairs(1)]
ODD = chip_pairs(1)
EVEN = chip_pairs(0)
SWAP_H = swap_pairs("h")
SWAP_CORE = swap_pairs("core")


def send(value, pairs):
    return lax.ppermute(value, AXES, pairs)


def tap_matrix(kernel, taps):
    count = kernel.shape[1]
    onehot = (taps[:, :, None] == jnp.arange(count, dtype=jnp.int32)).astype(jnp.float32)
    return jnp.einsum("ijk,uk->uij", onehot, kernel, precision=HIGHEST)


def by_h(own, other, h):
    return jnp.where(h == 0, jnp.concatenate([own, other], 1), jnp.concatenate([other, own], 1))


def body(estimate, observed, psf_taps, intersection):
    rows = intersection.shape[1] * TX
    full_width = observed.shape[2]
    depth = observed.shape[3]
    view_index = lax.axis_index("view")
    col_index = lax.axis_index("col")
    h, x = view_index // 4, view_index % 4
    column, k = col_index // 2, col_index % 2
    p = (x + column % 4) % 4
    core = k
    first_row = column * (4 * SLAB) + p * SLAB
    taps = psf_taps.shape[2]
    half = (taps - 1) // 2

    def piece(block, turn):
        return lax.dynamic_slice_in_dim(block, SLAB * ((x + turn) % 2), SLAB, 0)

    even = p % 2 == 0
    est = [send(piece(estimate, turn), SPREAD[turn]) for turn in (0, 1)]
    quarter = jnp.where(even, jnp.concatenate(est, 1), jnp.concatenate(est[::-1], 1))
    current = by_h(quarter, send(quarter, SWAP_H), h)
    images = [piece(observed[0], turn) for turn in (0, 1)]
    *images, _ = lax.optimization_barrier((*images, quarter))
    images = [send(image, route) for image, route in zip(images, SPREAD)]
    current, images[0] = lax.optimization_barrier((current, images[0]))

    kernels = psf_taps / jnp.sum(psf_taps, axis=2, keepdims=True)
    views = jnp.arange(kernels.shape[0], dtype=jnp.int32)
    own_views = 4 * h + 2 * core + jnp.stack([p % 2, (p + 1) % 2])
    picker = (own_views[:, None] == views[None, :]).astype(jnp.float32)
    own = jnp.einsum("uv,vdk->udk", picker, kernels, precision=HIGHEST)
    quarters = jnp.stack([core, 2 + core, 1 - core, 3 - core])
    quarter_width = full_width // 4
    local_y = (quarters[:, None] * quarter_width + jnp.arange(quarter_width, dtype=jnp.int32)[None, :]).reshape(-1)
    all_y = jnp.arange(full_width, dtype=jnp.int32)
    all_z = jnp.arange(depth, dtype=jnp.int32)
    slab = jnp.arange(SLAB, dtype=jnp.int32)
    side = jnp.where(even, SLAB, -SLAB)
    wide = jnp.concatenate([slab - side, slab, slab + side])
    mat_x = tap_matrix(own[:, 0], wide[None, :] - slab[:, None] + half)
    mat_y = tap_matrix(own[:, 1], local_y[None, :] - all_y[:, None] + half)
    mat_z = tap_matrix(own[:, 2], all_z[:, None] - all_z[None, :] + half)

    wide_rows = first_row + wide
    tile = (wide_rows // TX)[:, None] == jnp.arange(intersection.shape[1], dtype=jnp.int32)[None, :]
    tile = jnp.logical_and(tile, jnp.logical_and(wide_rows >= 0, wide_rows < rows)[:, None]).astype(jnp.float32)
    masks = jnp.einsum("vt,jt->vj", intersection.astype(jnp.float32), tile, precision=HIGHEST)
    weight_rows = jnp.einsum(
        "vrj,vj->vr", tap_matrix(kernels[:, 0], slab[:, None] - wide[None, :] + half), masks, precision=HIGHEST
    )

    def coverage(kernel, places, length):
        source = places[:, None] - jnp.arange(taps, dtype=jnp.int32)[None, :] + half
        inside = jnp.logical_and(source >= 0, source < length).astype(jnp.float32)
        return jnp.einsum("yk,vk->vy", inside, kernel, precision=HIGHEST)

    weight_cols = coverage(kernels[:, 1], local_y[: 2 * quarter_width], full_width)
    weight_depth = coverage(kernels[:, 2], all_z, depth)
    weight_plane = weight_rows[:, :, None] * weight_cols[:, None, :]
    weights = jnp.einsum("vxy,vz->xyz", weight_plane, weight_depth, precision=HIGHEST)
    own_masks = jnp.einsum("uv,vj->uj", picker, masks[:, SLAB : 2 * SLAB], precision=HIGHEST)
    inside = own_masks[:, :, None, None] > 0

    width = 2 * quarter_width
    scale = 1.0 / (weights + 1.0)
    for iteration in range(ITERS):
        extended = jnp.concatenate([send(current, ODD), current, send(current, EVEN)], 0)
        if iteration == 0:
            extended, images[1] = lax.optimization_barrier((extended, images[1]))
            images = jnp.stack(images)
        extended = jnp.concatenate([extended, send(extended, SWAP_CORE)], 1)
        blurred = jnp.einsum("urj,jyz->uryz", mat_x, extended, precision=HIGH)
        blurred = jnp.einsum("urjz,uyj->uryz", blurred, mat_y, precision=HIGH)
        blurred = jnp.einsum("uryz,uzw->uryw", blurred, mat_z, precision=HIGH)
        ratio = jnp.where(inside, images / jnp.where(inside, blurred, 1.0), 0.0)
        back = jnp.einsum("uryw,uzw->uryz", ratio, mat_z, precision=HIGH)
        back = jnp.einsum("uryz,uyj->urjz", back, mat_y, precision=HIGH)
        back = jnp.einsum("urj,uryz->jyz", mat_x, back, precision=HIGH)
        part = back[:, :width] + send(back[:, width:], SWAP_CORE)
        part = part[SLAB : 2 * SLAB] + send(part[:SLAB], ODD) + send(part[2 * SLAB :], EVEN)
        if iteration < ITERS - 1:
            current = current * (part + send(part, SWAP_H) + 1.0) * scale

    def own_half(value, mine):
        return jnp.where((h == 0) == mine, value[:, :quarter_width], value[:, quarter_width:])

    total = own_half(part, True) + send(own_half(part, False), SWAP_H)
    quarter = own_half(current, True) * (total + 1.0) * own_half(scale, True)

    block = quarter_width // 2
    first, second = quarter[:, :block], quarter[:, block:]
    chosen = [jnp.where(even, first, second), jnp.where(even, second, first)]
    one, two = (send(value, reverse(route)) for value, route in zip(chosen, SPREAD))
    return jnp.where(x % 2 == 0, jnp.concatenate([one, two], 0), jnp.concatenate([two, one], 0))


def solution(mesh):
    return jax.shard_map(
        body,
        mesh=mesh,
        in_specs=(P("col", "view", None), P("view", "col", None, None), P(), P()),
        out_specs=P("col", "view", None),
        check_vma=False,
    )
```

```python
import jax
import jax.numpy as jnp
from jax import lax
from jax.sharding import PartitionSpec as P

TX = 128
ITERS = 2
HIGH = lax.Precision.HIGH
HIGHEST = lax.Precision.HIGHEST
AXES = ("view", "col")
SLAB = 16
COLS = 64


def device(h, x, c):
    return (h * 4 + x) * COLS + c


def chip_x(column, p):
    return (p - column % 4) % 4


def spread_pairs(turn):
    pairs = []
    for h in range(2):
        for column in range(COLS // 2):
            for x in range(4):
                for k in range(2):
                    p = 2 * k + (x + turn) % 2
                    pairs.append(
                        (
                            device(h, x, 2 * column + k),
                            device(h, chip_x(column, p), 2 * column + x // 2),
                        )
                    )
    return pairs


def chip_pairs(first):
    pairs = []
    for h in range(2):
        for chip in range(first, COLS // 2 * 4 - 1, 2):
            for core in range(2):
                low, high = (
                    device((h + q // 16) % 2, chip_x(q // 4, q % 4), 2 * (q // 4) + core)
                    for q in (chip, chip + 1)
                )
                pairs += [(low, high), (high, low)]
    return pairs


def swap_pairs(across):
    pairs = []
    for h in range(2):
        for x in range(4):
            for c in range(COLS):
                other = device(1 - h, x, c) if across == "h" else device(h, x, c ^ 1)
                pairs.append((device(h, x, c), other))
    return pairs


def reverse(pairs):
    return [(b, a) for a, b in pairs]


SPREAD = [spread_pairs(0), spread_pairs(1)]
ODD = chip_pairs(1)
EVEN = chip_pairs(0)
SWAP_H = swap_pairs("h")
SWAP_CORE = swap_pairs("core")


def send(value, pairs):
    return lax.ppermute(value, AXES, pairs)


def tap_matrix(kernel, taps):
    count = kernel.shape[1]
    onehot = (taps[:, :, None] == jnp.arange(count, dtype=jnp.int32)).astype(jnp.float32)
    return jnp.einsum("ijk,uk->uij", onehot, kernel, precision=HIGHEST)


def by_h(own, other, h):
    return jnp.where(h == 0, jnp.concatenate([own, other], 0), jnp.concatenate([other, own], 0))


def body(estimate, observed, psf_taps, intersection):
    rows = intersection.shape[1] * TX
    full_width = observed.shape[2]
    depth = observed.shape[3]
    view_index = lax.axis_index("view")
    col_index = lax.axis_index("col")
    h, x = view_index // 4, view_index % 4
    column, k = col_index // 2, col_index % 2
    p = (x + column % 4) % 4
    core = k
    first_row = column * (4 * SLAB) + p * SLAB
    taps = psf_taps.shape[2]
    half = (taps - 1) // 2

    def piece(value, turn, axis):
        return lax.dynamic_slice_in_dim(value, SLAB * ((x + turn) % 2), SLAB, axis)

    def ordered(pair, first):
        one, two = pair
        return jnp.where(first, one, two), jnp.where(first, two, one)

    even = p % 2 == 0
    flipped = jnp.swapaxes(estimate, 0, 1)
    both = by_h(flipped, send(flipped, SWAP_H), h)
    current = jnp.concatenate(
        ordered([send(piece(both, turn, 1), SPREAD[turn]) for turn in (0, 1)], even), 0
    )
    images = [send(piece(observed[0], turn, 0), SPREAD[turn]) for turn in (0, 1)]
    psf_taps, intersection, current = lax.optimization_barrier((psf_taps, intersection, current))

    kernels = psf_taps / jnp.sum(psf_taps, axis=2, keepdims=True)
    views = jnp.arange(kernels.shape[0], dtype=jnp.int32)
    own_views = 4 * h + 2 * core + jnp.stack([p % 2, (p + 1) % 2])
    picker = (own_views[:, None] == views[None, :]).astype(jnp.float32)
    own = jnp.einsum("uv,vdk->udk", picker, kernels, precision=HIGHEST)
    width = full_width // 2
    block = estimate.shape[1]
    place = jnp.arange(width, dtype=jnp.int32)
    place = place // (2 * block) * block + place // block % 2 * width + place % block
    local_y = jnp.concatenate([place + core * (width // 2), place + (1 - core) * (width // 2)])
    all_y = jnp.arange(full_width, dtype=jnp.int32)
    all_z = jnp.arange(depth, dtype=jnp.int32)
    slab = jnp.arange(SLAB, dtype=jnp.int32)
    side = jnp.where(even, SLAB, -SLAB)
    wide = jnp.concatenate([slab - side, slab, slab + side])
    mat_x = tap_matrix(own[:, 0], wide[None, :] - slab[:, None] + half)
    mat_y = tap_matrix(own[:, 1], local_y[None, :] - all_y[:, None] + half)
    mat_z = tap_matrix(own[:, 2], all_z[:, None] - all_z[None, :] + half)

    wide_rows = first_row + wide
    tile = (wide_rows // TX)[:, None] == jnp.arange(intersection.shape[1], dtype=jnp.int32)[None, :]
    tile = jnp.logical_and(tile, jnp.logical_and(wide_rows >= 0, wide_rows < rows)[:, None]).astype(jnp.float32)
    masks = jnp.einsum("vt,jt->vj", intersection.astype(jnp.float32), tile, precision=HIGHEST)
    weight_rows = jnp.einsum(
        "vrj,vj->vr", tap_matrix(kernels[:, 0], slab[:, None] - wide[None, :] + half), masks, precision=HIGHEST
    )

    def coverage(kernel, places, length):
        source = places[:, None] - jnp.arange(taps, dtype=jnp.int32)[None, :] + half
        inside = jnp.logical_and(source >= 0, source < length).astype(jnp.float32)
        return jnp.einsum("yk,vk->vy", inside, kernel, precision=HIGHEST)

    weight_cols = coverage(kernels[:, 1], local_y[:width], full_width)
    weight_depth = coverage(kernels[:, 2], all_z, depth)
    weight_plane = weight_cols[:, :, None] * weight_rows[:, None, :]
    weights = jnp.einsum("vyx,vz->yxz", weight_plane, weight_depth, precision=HIGHEST)
    own_masks = jnp.einsum("uv,vj->uj", picker, masks[:, SLAB : 2 * SLAB], precision=HIGHEST)
    inside = own_masks[:, :, None, None] > 0

    scale = 1.0 / (weights + 1.0)
    for iteration in range(ITERS):
        extended = jnp.concatenate([send(current, ODD), current, send(current, EVEN)], 1)
        if iteration == 0:
            extended, scale, inside, mat_x, mat_y, mat_z, *images = lax.optimization_barrier(
                (extended, scale, inside, mat_x, mat_y, mat_z, *images)
            )
            images = jnp.stack(images)
        extended = jnp.concatenate([extended, send(extended, SWAP_CORE)], 0)
        blurred = jnp.einsum("urj,yjz->uryz", mat_x, extended, precision=HIGH)
        blurred = jnp.einsum("urjz,uyj->uryz", blurred, mat_y, precision=HIGH)
        blurred = jnp.einsum("uryz,uzw->uryw", blurred, mat_z, precision=HIGH)
        ratio = jnp.where(inside, images / jnp.where(inside, blurred, 1.0), 0.0)
        back = jnp.einsum("uryw,uzw->uryz", ratio, mat_z, precision=HIGH)
        back = jnp.einsum("uryz,uyj->urjz", back, mat_y, precision=HIGH)
        back = jnp.einsum("urj,uryz->yjz", mat_x, back, precision=HIGH)
        part = back[:width] + send(back[width:], SWAP_CORE)
        part = part[:, SLAB : 2 * SLAB] + send(part[:, :SLAB], ODD) + send(part[:, 2 * SLAB :], EVEN)
        if iteration < ITERS - 1:
            current = current * (part + send(part, SWAP_H) + 1.0) * scale

    own_h = (place // width == h)[:, None, None]
    terms = current * scale * jnp.where(own_h, part + 1.0, part)
    terms = ordered([terms[: 2 * block], terms[2 * block :]], even)
    terms = [send(value, reverse(route)) for value, route in zip(terms, SPREAD)]
    terms = jnp.concatenate(ordered(terms, x % 2 == 0), 1)
    mine, other = ordered([terms[:block], terms[block:]], h == 0)
    return jnp.swapaxes(mine + send(other, SWAP_H), 0, 1)


def solution(mesh):
    return jax.shard_map(
        body,
        mesh=mesh,
        in_specs=(P("col", "view", None), P("view", "col", None, None), P(), P()),
        out_specs=P("col", "view", None),
        check_vma=False,
    )
```

```python
import jax
import jax.numpy as jnp
from jax import lax
from jax.sharding import PartitionSpec as P

TX = 128
ITERS = 2
HIGH = lax.Precision.HIGH
HIGHEST = lax.Precision.HIGHEST
AXES = ("view", "col")
SLAB = 16
COLS = 64


def device(h, x, c):
    return (h * 4 + x) * COLS + c


def chip_x(column, p):
    return (p - column % 4) % 4


def spread_pairs(turn):
    pairs = []
    for h in range(2):
        for column in range(COLS // 2):
            for x in range(4):
                for k in range(2):
                    p = 2 * k + (x + turn) % 2
                    pairs.append(
                        (
                            device(h, x, 2 * column + k),
                            device(h, chip_x(column, p), 2 * column + x // 2),
                        )
                    )
    return pairs


def chip_pairs(first):
    pairs = []
    for h in range(2):
        for chip in range(first, COLS // 2 * 4 - 1, 2):
            for core in range(2):
                low, high = (
                    device((h + q // 16) % 2, chip_x(q // 4, q % 4), 2 * (q // 4) + core)
                    for q in (chip, chip + 1)
                )
                pairs += [(low, high), (high, low)]
    return pairs


def swap_pairs(across):
    pairs = []
    for h in range(2):
        for x in range(4):
            for c in range(COLS):
                other = device(1 - h, x, c) if across == "h" else device(h, x, c ^ 1)
                pairs.append((device(h, x, c), other))
    return pairs


def reverse(pairs):
    return [(b, a) for a, b in pairs]


SPREAD = [spread_pairs(0), spread_pairs(1)]
ODD = chip_pairs(1)
EVEN = chip_pairs(0)
SWAP_H = swap_pairs("h")
SWAP_CORE = swap_pairs("core")


def send(value, pairs):
    return lax.ppermute(value, AXES, pairs)


def tap_matrix(kernel, taps):
    count = kernel.shape[1]
    onehot = (taps[:, :, None] == jnp.arange(count, dtype=jnp.int32)).astype(jnp.float32)
    return jnp.einsum("ijk,uk->uij", onehot, kernel, precision=HIGHEST)


def by_h(own, other, h):
    return jnp.where(h == 0, jnp.concatenate([own, other], 0), jnp.concatenate([other, own], 0))


def body(estimate, observed, psf_taps, intersection):
    rows = intersection.shape[1] * TX
    full_width = observed.shape[2]
    depth = observed.shape[3]
    view_index = lax.axis_index("view")
    col_index = lax.axis_index("col")
    h, x = view_index // 4, view_index % 4
    column, k = col_index // 2, col_index % 2
    p = (x + column % 4) % 4
    core = k
    first_row = column * (4 * SLAB) + p * SLAB
    taps = psf_taps.shape[2]
    half = (taps - 1) // 2

    def piece(value, turn, axis):
        return lax.dynamic_slice_in_dim(value, SLAB * ((x + turn) % 2), SLAB, axis)

    def ordered(pair, first):
        one, two = pair
        return jnp.where(first, one, two), jnp.where(first, two, one)

    even = p % 2 == 0
    flipped = jnp.swapaxes(estimate, 0, 1)
    both = by_h(flipped, send(flipped, SWAP_H), h)
    current = jnp.concatenate(
        ordered([send(piece(both, turn, 1), SPREAD[turn]) for turn in (0, 1)], even), 0
    )
    images = [piece(observed[0], turn, 0) for turn in (0, 1)]
    *others, _ = lax.optimization_barrier((*images, both))
    images = [send(image, SPREAD[turn]) for turn, image in enumerate(images)] + [
        send(send(image, SWAP_H), SPREAD[turn]) for turn, image in enumerate(others)
    ]
    psf_taps, intersection, current, *images[:2] = lax.optimization_barrier(
        (psf_taps, intersection, current, *images[:2])
    )

    kernels = psf_taps / jnp.sum(psf_taps, axis=2, keepdims=True)
    views = jnp.arange(kernels.shape[0], dtype=jnp.int32)
    own_views = 2 * core + jnp.stack([4 * g + turn for g in (h, 1 - h) for turn in (p % 2, (p + 1) % 2)])
    picker = (own_views[:, None] == views[None, :]).astype(jnp.float32)
    own = jnp.einsum("uv,vdk->udk", picker, kernels, precision=HIGHEST)
    width = full_width // 2
    block = estimate.shape[1]
    place = jnp.arange(width, dtype=jnp.int32)
    place = place // (2 * block) * block + place // block % 2 * width + place % block
    local_y = jnp.concatenate([place + core * (width // 2), place + (1 - core) * (width // 2)])
    all_y = jnp.arange(full_width, dtype=jnp.int32)
    all_z = jnp.arange(depth, dtype=jnp.int32)
    slab = jnp.arange(SLAB, dtype=jnp.int32)
    side = jnp.where(even, SLAB, -SLAB)
    wide = jnp.concatenate([slab - side, slab, slab + side])
    mat_x = tap_matrix(own[:, 0], wide[None, :] - slab[:, None] + half)
    mat_y = tap_matrix(own[:, 1], local_y[None, :] - all_y[:, None] + half)
    mat_z = tap_matrix(own[:, 2], all_z[:, None] - all_z[None, :] + half)

    wide_rows = first_row + wide
    tile = (wide_rows // TX)[:, None] == jnp.arange(intersection.shape[1], dtype=jnp.int32)[None, :]
    tile = jnp.logical_and(tile, jnp.logical_and(wide_rows >= 0, wide_rows < rows)[:, None]).astype(jnp.float32)
    masks = jnp.einsum("vt,jt->vj", intersection.astype(jnp.float32), tile, precision=HIGHEST)
    weight_rows = jnp.einsum(
        "vrj,vj->vr", tap_matrix(kernels[:, 0], slab[:, None] - wide[None, :] + half), masks, precision=HIGHEST
    )

    def coverage(kernel, places, length):
        source = places[:, None] - jnp.arange(taps, dtype=jnp.int32)[None, :] + half
        inside = jnp.logical_and(source >= 0, source < length).astype(jnp.float32)
        return jnp.einsum("yk,vk->vy", inside, kernel, precision=HIGHEST)

    weight_cols = coverage(kernels[:, 1], local_y[:width], full_width)
    weight_depth = coverage(kernels[:, 2], all_z, depth)
    weight_plane = weight_cols[:, :, None] * weight_rows[:, None, :]
    weights = jnp.einsum("vyx,vz->yxz", weight_plane, weight_depth, precision=HIGHEST)
    own_masks = jnp.einsum("uv,vj->uj", picker, masks[:, SLAB : 2 * SLAB], precision=HIGHEST)
    inside = own_masks[:, :, None, None] > 0

    scale = 1.0 / (weights + 1.0)
    for iteration in range(ITERS):
        extended = jnp.concatenate([send(current, ODD), current, send(current, EVEN)], 1)
        if iteration == 0:
            extended, scale, inside, mat_x, mat_y, mat_z, *images[:3] = lax.optimization_barrier(
                (extended, scale, inside, mat_x, mat_y, mat_z, *images[:3])
            )
        swapped = send(extended, SWAP_CORE)
        if iteration == 0:
            swapped, images[3] = lax.optimization_barrier((swapped, images[3]))
            images = jnp.stack(images)
        extended = jnp.concatenate([extended, swapped], 0)
        blurred = jnp.einsum("urj,yjz->uryz", mat_x, extended, precision=HIGH)
        blurred = jnp.einsum("urjz,uyj->uryz", blurred, mat_y, precision=HIGH)
        blurred = jnp.einsum("uryz,uzw->uryw", blurred, mat_z, precision=HIGH)
        ratio = jnp.where(inside, images / jnp.where(inside, blurred, 1.0), 0.0)
        back = jnp.einsum("uryw,uzw->uryz", ratio, mat_z, precision=HIGH)
        back = jnp.einsum("uryz,uyj->urjz", back, mat_y, precision=HIGH)
        back = jnp.einsum("urj,uryz->yjz", mat_x, back, precision=HIGH)
        part = back[:width] + send(back[width:], SWAP_CORE)
        part = part[:, SLAB : 2 * SLAB] + send(part[:, :SLAB], ODD) + send(part[:, 2 * SLAB :], EVEN)
        if iteration < ITERS - 1:
            current = current * (part + 1.0) * scale

    def own_half(value):
        value = value.reshape(2, 2, block, SLAB, depth)
        return jnp.where(h == 0, value[:, 0], value[:, 1])

    result = own_half(current) * (own_half(part) + 1.0) * own_half(scale)
    result = ordered([result[0], result[1]], even)
    result = [send(value, reverse(route)) for value, route in zip(result, SPREAD)]
    return jnp.swapaxes(jnp.concatenate(ordered(result, x % 2 == 0), 1), 0, 1)


def solution(mesh):
    return jax.shard_map(
        body,
        mesh=mesh,
        in_specs=(P("col", "view", None), P("view", "col", None, None), P(), P()),
        out_specs=P("col", "view", None),
        check_vma=False,
    )
```

```python
import jax
import jax.numpy as jnp
from jax import lax
from jax.sharding import PartitionSpec as P

TX = 128
ITERS = 2
HIGH = lax.Precision.HIGH
HIGHEST = lax.Precision.HIGHEST
AXES = ("view", "col")
SLAB = 16
COLS = 64


def device(h, x, c):
    return (h * 4 + x) * COLS + c


def chip_x(column, p):
    return (p - column % 4) % 4


def spread_pairs(turn):
    pairs = []
    for h in range(2):
        for column in range(COLS // 2):
            for x in range(4):
                for k in range(2):
                    p = 2 * k + (x + turn) % 2
                    pairs.append(
                        (
                            device(h, x, 2 * column + k),
                            device(h, chip_x(column, p), 2 * column + x // 2),
                        )
                    )
    return pairs


def chip_pairs(first):
    pairs = []
    for h in range(2):
        for chip in range(first, COLS // 2 * 4 - 1, 2):
            for core in range(2):
                low, high = (
                    device((h + q // 16) % 2, chip_x(q // 4, q % 4), 2 * (q // 4) + core)
                    for q in (chip, chip + 1)
                )
                pairs += [(low, high), (high, low)]
    return pairs


def swap_pairs(across):
    pairs = []
    for h in range(2):
        for x in range(4):
            for c in range(COLS):
                other = device(1 - h, x, c) if across == "h" else device(h, x, c ^ 1)
                pairs.append((device(h, x, c), other))
    return pairs


def reverse(pairs):
    return [(b, a) for a, b in pairs]


SPREAD = [spread_pairs(0), spread_pairs(1)]
ODD = chip_pairs(1)
EVEN = chip_pairs(0)
SWAP_H = swap_pairs("h")
SWAP_CORE = swap_pairs("core")


def send(value, pairs):
    return lax.ppermute(value, AXES, pairs)


def tap_matrix(kernel, taps):
    count = kernel.shape[1]
    onehot = (taps[:, :, None] == jnp.arange(count, dtype=jnp.int32)).astype(jnp.float32)
    return jnp.einsum("ijk,uk->uij", onehot, kernel, precision=HIGHEST)


def by_h(own, other, h):
    return jnp.where(h == 0, jnp.concatenate([own, other], 0), jnp.concatenate([other, own], 0))


def body(estimate, observed, psf_taps, intersection):
    rows = intersection.shape[1] * TX
    full_width = observed.shape[2]
    depth = observed.shape[3]
    view_index = lax.axis_index("view")
    col_index = lax.axis_index("col")
    h, x = view_index // 4, view_index % 4
    column, k = col_index // 2, col_index % 2
    p = (x + column % 4) % 4
    core = k
    first_row = column * (4 * SLAB) + p * SLAB
    taps = psf_taps.shape[2]
    half = (taps - 1) // 2

    def piece(value, turn, axis):
        return lax.dynamic_slice_in_dim(value, SLAB * ((x + turn) % 2), SLAB, axis)

    def ordered(pair, first):
        one, two = pair
        return jnp.where(first, one, two), jnp.where(first, two, one)

    even = p % 2 == 0
    flipped = jnp.swapaxes(estimate, 0, 1)
    quarter = jnp.concatenate(
        ordered([send(piece(flipped, turn, 1), SPREAD[turn]) for turn in (0, 1)], even), 0
    )
    current = by_h(quarter, send(quarter, SWAP_H), h)
    images = [piece(observed[0], turn, 0) for turn in (0, 1)]
    *images, _ = lax.optimization_barrier((*images, quarter))
    images = [send(image, SPREAD[turn]) for turn, image in enumerate(images)]
    psf_taps, intersection, current = lax.optimization_barrier((psf_taps, intersection, current))

    kernels = psf_taps / jnp.sum(psf_taps, axis=2, keepdims=True)
    views = jnp.arange(kernels.shape[0], dtype=jnp.int32)
    own_views = 4 * h + 2 * core + jnp.stack([p % 2, (p + 1) % 2])
    picker = (own_views[:, None] == views[None, :]).astype(jnp.float32)
    own = jnp.einsum("uv,vdk->udk", picker, kernels, precision=HIGHEST)
    width = full_width // 2
    block = estimate.shape[1]
    place = jnp.arange(width, dtype=jnp.int32)
    place = place // (2 * block) * width + place % (2 * block)
    local_y = jnp.concatenate([place + core * (width // 2), place + (1 - core) * (width // 2)])
    all_y = jnp.arange(full_width, dtype=jnp.int32)
    all_z = jnp.arange(depth, dtype=jnp.int32)
    slab = jnp.arange(SLAB, dtype=jnp.int32)
    side = jnp.where(even, SLAB, -SLAB)
    wide = jnp.concatenate([slab - side, slab, slab + side])
    mat_x = tap_matrix(own[:, 0], wide[None, :] - slab[:, None] + half)
    mat_y = tap_matrix(own[:, 1], local_y[None, :] - all_y[:, None] + half)
    mat_z = tap_matrix(own[:, 2], all_z[:, None] - all_z[None, :] + half)

    wide_rows = first_row + wide
    tile = (wide_rows // TX)[:, None] == jnp.arange(intersection.shape[1], dtype=jnp.int32)[None, :]
    tile = jnp.logical_and(tile, jnp.logical_and(wide_rows >= 0, wide_rows < rows)[:, None]).astype(jnp.float32)
    masks = jnp.einsum("vt,jt->vj", intersection.astype(jnp.float32), tile, precision=HIGHEST)
    weight_rows = jnp.einsum(
        "vrj,vj->vr", tap_matrix(kernels[:, 0], slab[:, None] - wide[None, :] + half), masks, precision=HIGHEST
    )

    def coverage(kernel, places, length):
        source = places[:, None] - jnp.arange(taps, dtype=jnp.int32)[None, :] + half
        inside = jnp.logical_and(source >= 0, source < length).astype(jnp.float32)
        return jnp.einsum("yk,vk->vy", inside, kernel, precision=HIGHEST)

    weight_cols = coverage(kernels[:, 1], local_y[:width], full_width)
    weight_depth = coverage(kernels[:, 2], all_z, depth)
    weight_plane = weight_cols[:, :, None] * weight_rows[:, None, :]
    weights = jnp.einsum("vyx,vz->yxz", weight_plane, weight_depth, precision=HIGHEST)
    own_masks = jnp.einsum("uv,vj->uj", picker, masks[:, SLAB : 2 * SLAB], precision=HIGHEST)
    inside = own_masks[:, :, None, None] > 0

    scale = 1.0 / (weights + 1.0)
    for iteration in range(ITERS):
        extended = jnp.concatenate([send(current, ODD), current, send(current, EVEN)], 1)
        if iteration == 0:
            extended, scale, inside, mat_x, mat_y, mat_z, *images = lax.optimization_barrier(
                (extended, scale, inside, mat_x, mat_y, mat_z, *images)
            )
            images = jnp.stack(images)
        extended = jnp.concatenate([extended, send(extended, SWAP_CORE)], 0)
        blurred = jnp.einsum("urj,yjz->uryz", mat_x, extended, precision=HIGH)
        blurred = jnp.einsum("urjz,uyj->uryz", blurred, mat_y, precision=HIGH)
        blurred = jnp.einsum("uryz,uzw->uryw", blurred, mat_z, precision=HIGH)
        ratio = jnp.where(inside, images / jnp.where(inside, blurred, 1.0), 0.0)
        back = jnp.einsum("uryw,uzw->uryz", ratio, mat_z, precision=HIGH)
        back = jnp.einsum("uryz,uyj->urjz", back, mat_y, precision=HIGH)
        back = jnp.einsum("urj,uryz->yjz", mat_x, back, precision=HIGH)
        part = back[:width] + send(back[width:], SWAP_CORE)
        part = part[:, SLAB : 2 * SLAB] + send(part[:, :SLAB], ODD) + send(part[:, 2 * SLAB :], EVEN)
        if iteration < ITERS - 1:
            current = current * (part + send(part, SWAP_H) + 1.0) * scale

    def own_half(value, mine):
        return jnp.where((h == 0) == mine, value[: 2 * block], value[2 * block :])

    total = own_half(part, True) + send(own_half(part, False), SWAP_H)
    quarter = own_half(current, True) * (total + 1.0) * own_half(scale, True)

    result = ordered([quarter[:block], quarter[block:]], even)
    result = [send(value, reverse(route)) for value, route in zip(result, SPREAD)]
    return jnp.swapaxes(jnp.concatenate(ordered(result, x % 2 == 0), 1), 0, 1)


def solution(mesh):
    return jax.shard_map(
        body,
        mesh=mesh,
        in_specs=(P("col", "view", None), P("view", "col", None, None), P(), P()),
        out_specs=P("col", "view", None),
        check_vma=False,
    )
```

```python
import jax
import jax.numpy as jnp
from jax import lax
from jax.sharding import PartitionSpec as P

TX = 128
ITERS = 2
HIGH = lax.Precision.HIGH
HIGHEST = lax.Precision.HIGHEST
AXES = ("view", "col")
SLAB = 16
COLS = 64


def device(h, x, c):
    return (h * 4 + x) * COLS + c


def chip_x(column, p):
    return (p - column % 4) % 4


def spread_pairs(turn):
    pairs = []
    for h in range(2):
        for column in range(COLS // 2):
            for x in range(4):
                for k in range(2):
                    p = 2 * k + (x + turn) % 2
                    pairs.append(
                        (
                            device(h, x, 2 * column + k),
                            device(h, chip_x(column, p), 2 * column + x // 2),
                        )
                    )
    return pairs


def chip_pairs(first):
    pairs = []
    for h in range(2):
        for chip in range(first, COLS // 2 * 4 - 1, 2):
            for core in range(2):
                low, high = (
                    device((h + q // 16) % 2, chip_x(q // 4, q % 4), 2 * (q // 4) + core)
                    for q in (chip, chip + 1)
                )
                pairs += [(low, high), (high, low)]
    return pairs


def swap_pairs(across):
    pairs = []
    for h in range(2):
        for x in range(4):
            for c in range(COLS):
                other = device(1 - h, x, c) if across == "h" else device(h, x, c ^ 1)
                pairs.append((device(h, x, c), other))
    return pairs


def reverse(pairs):
    return [(b, a) for a, b in pairs]


SPREAD = [spread_pairs(0), spread_pairs(1)]
ODD = chip_pairs(1)
EVEN = chip_pairs(0)
SWAP_H = swap_pairs("h")
SWAP_CORE = swap_pairs("core")


def send(value, pairs):
    return lax.ppermute(value, AXES, pairs)


def tap_matrix(kernel, taps):
    count = kernel.shape[1]
    onehot = (taps[:, :, None] == jnp.arange(count, dtype=jnp.int32)).astype(jnp.float32)
    return jnp.einsum("ijk,uk->uij", onehot, kernel, precision=HIGHEST)


def by_h(own, other, h):
    return jnp.where(h == 0, jnp.concatenate([own, other], 0), jnp.concatenate([other, own], 0))


def body(estimate, observed, psf_taps, intersection):
    rows = intersection.shape[1] * TX
    full_width = observed.shape[2]
    depth = observed.shape[3]
    view_index = lax.axis_index("view")
    col_index = lax.axis_index("col")
    h, x = view_index // 4, view_index % 4
    column, k = col_index // 2, col_index % 2
    p = (x + column % 4) % 4
    core = k
    first_row = column * (4 * SLAB) + p * SLAB
    taps = psf_taps.shape[2]
    half = (taps - 1) // 2

    def piece(value, turn, axis):
        return lax.dynamic_slice_in_dim(value, SLAB * ((x + turn) % 2), SLAB, axis)

    def ordered(pair, first):
        one, two = pair
        return jnp.where(first, one, two), jnp.where(first, two, one)

    even = p % 2 == 0
    flipped = jnp.swapaxes(estimate, 0, 1)
    quarter = jnp.concatenate(
        ordered([send(piece(flipped, turn, 1), SPREAD[turn]) for turn in (0, 1)], even), 0
    )
    current = by_h(quarter, send(quarter, SWAP_H), h)
    images = [piece(observed[0], turn, 0) for turn in (0, 1)]
    images[1], _ = lax.optimization_barrier((images[1], quarter))
    images = [send(image, SPREAD[turn]) for turn, image in enumerate(images)]
    psf_taps, intersection, current = lax.optimization_barrier((psf_taps, intersection, current))

    kernels = psf_taps / jnp.sum(psf_taps, axis=2, keepdims=True)
    views = jnp.arange(kernels.shape[0], dtype=jnp.int32)
    own_views = 4 * h + 2 * core + jnp.stack([p % 2, (p + 1) % 2])
    picker = (own_views[:, None] == views[None, :]).astype(jnp.float32)
    own = jnp.einsum("uv,vdk->udk", picker, kernels, precision=HIGHEST)
    width = full_width // 2
    block = estimate.shape[1]
    place = jnp.arange(width, dtype=jnp.int32)
    place = place // (2 * block) * width + place % (2 * block)
    local_y = jnp.concatenate([place + core * (width // 2), place + (1 - core) * (width // 2)])
    all_y = jnp.arange(full_width, dtype=jnp.int32)
    all_z = jnp.arange(depth, dtype=jnp.int32)
    slab = jnp.arange(SLAB, dtype=jnp.int32)
    side = jnp.where(even, SLAB, -SLAB)
    wide = jnp.concatenate([slab - side, slab, slab + side])
    mat_x = tap_matrix(own[:, 0], wide[None, :] - slab[:, None] + half)
    mat_y = tap_matrix(own[:, 1], local_y[None, :] - all_y[:, None] + half)
    mat_z = tap_matrix(own[:, 2], all_z[:, None] - all_z[None, :] + half)

    wide_rows = first_row + wide
    tile = (wide_rows // TX)[:, None] == jnp.arange(intersection.shape[1], dtype=jnp.int32)[None, :]
    tile = jnp.logical_and(tile, jnp.logical_and(wide_rows >= 0, wide_rows < rows)[:, None]).astype(jnp.float32)
    masks = jnp.einsum("vt,jt->vj", intersection.astype(jnp.float32), tile, precision=HIGHEST)
    weight_rows = jnp.einsum(
        "vrj,vj->vr", tap_matrix(kernels[:, 0], slab[:, None] - wide[None, :] + half), masks, precision=HIGHEST
    )

    def coverage(kernel, places, length):
        source = places[:, None] - jnp.arange(taps, dtype=jnp.int32)[None, :] + half
        inside = jnp.logical_and(source >= 0, source < length).astype(jnp.float32)
        return jnp.einsum("yk,vk->vy", inside, kernel, precision=HIGHEST)

    weight_cols = coverage(kernels[:, 1], local_y[:width], full_width)
    weight_depth = coverage(kernels[:, 2], all_z, depth)
    weight_plane = weight_cols[:, :, None] * weight_rows[:, None, :]
    weights = jnp.einsum("vyx,vz->yxz", weight_plane, weight_depth, precision=HIGHEST)
    own_masks = jnp.einsum("uv,vj->uj", picker, masks[:, SLAB : 2 * SLAB], precision=HIGHEST)
    inside = own_masks[:, :, None, None] > 0

    scale = 1.0 / (weights + 1.0)
    for iteration in range(ITERS):
        extended = jnp.concatenate([send(current, ODD), current, send(current, EVEN)], 1)
        if iteration == 0:
            extended, scale, inside, mat_x, mat_y, mat_z, *images = lax.optimization_barrier(
                (extended, scale, inside, mat_x, mat_y, mat_z, *images)
            )
            images = lax.optimization_barrier(jnp.where(inside, jnp.stack(images), 0.0))
        extended = jnp.concatenate([extended, send(extended, SWAP_CORE)], 0)
        blurred = jnp.einsum("urj,yjz->uryz", mat_x, extended, precision=HIGH)
        blurred = jnp.einsum("urjz,uyj->uryz", blurred, mat_y, precision=HIGH)
        blurred = jnp.einsum("uryz,uzw->uryw", blurred, mat_z, precision=HIGH)
        ratio = images / jnp.where(inside, blurred, 1.0)
        back = jnp.einsum("uryw,uzw->uryz", ratio, mat_z, precision=HIGH)
        own_part, other_part = (
            jnp.einsum(
                "urj,uryz->yjz",
                mat_x,
                jnp.einsum("uryz,uyj->urjz", back, columns, precision=HIGH),
                precision=HIGH,
            )
            for columns in (mat_y[:, :, :width], mat_y[:, :, width:])
        )
        part = lax.optimization_barrier(own_part) + send(other_part, SWAP_CORE)
        part = part[:, SLAB : 2 * SLAB] + send(part[:, :SLAB], ODD) + send(part[:, 2 * SLAB :], EVEN)
        if iteration < ITERS - 1:
            current = current * (part + send(part, SWAP_H) + 1.0) * scale

    def own_half(value, mine):
        return jnp.where((h == 0) == mine, value[: 2 * block], value[2 * block :])

    total = own_half(part, True) + send(own_half(part, False), SWAP_H)
    quarter = own_half(current, True) * (total + 1.0) * own_half(scale, True)

    quarter = jnp.swapaxes(quarter, 0, 1)
    result = ordered([quarter[:, :block], quarter[:, block:]], even)
    result = lax.optimization_barrier(tuple(result))
    result = [send(value, reverse(route)) for value, route in zip(result, SPREAD)]
    return jnp.concatenate(ordered(result, x % 2 == 0), 0)


def solution(mesh):
    return jax.shard_map(
        body,
        mesh=mesh,
        in_specs=(P("col", "view", None), P("view", "col", None, None), P(), P()),
        out_specs=P("col", "view", None),
        check_vma=False,
    )
```

```python
import jax
import jax.numpy as jnp
from jax import lax
from jax.sharding import PartitionSpec as P

TX = 128
ITERS = 2
HIGH = lax.Precision.HIGH
HIGHEST = lax.Precision.HIGHEST
AXES = ("view", "col")
SLAB = 16
COLS = 64


def device(h, x, c):
    return (h * 4 + x) * COLS + c


def chip_x(column, p):
    return (p - column % 4) % 4


def spread_pairs(turn, cross=0):
    pairs = []
    for h in range(2):
        for column in range(COLS // 2):
            for x in range(4):
                for k in range(2):
                    p = 2 * k + (x + turn) % 2
                    pairs.append(
                        (
                            device(h, x, 2 * column + k),
                            device(h ^ cross, chip_x(column, p), 2 * column + x // 2),
                        )
                    )
    return pairs


def chip_pairs(first):
    pairs = []
    for h in range(2):
        for chip in range(first, COLS // 2 * 4 - 1, 2):
            for core in range(2):
                low, high = (
                    device((h + q // 16) % 2, chip_x(q // 4, q % 4), 2 * (q // 4) + core)
                    for q in (chip, chip + 1)
                )
                pairs += [(low, high), (high, low)]
    return pairs


def swap_pairs(across):
    pairs = []
    for h in range(2):
        for x in range(4):
            for c in range(COLS):
                other = device(1 - h, x, c) if across == "h" else device(h, x, c ^ 1)
                pairs.append((device(h, x, c), other))
    return pairs


def reverse(pairs):
    return [(b, a) for a, b in pairs]


SPREAD = [spread_pairs(0), spread_pairs(1)]
CROSS = [spread_pairs(0, 1), spread_pairs(1, 1)]
ODD = chip_pairs(1)
EVEN = chip_pairs(0)
SWAP_H = swap_pairs("h")
SWAP_CORE = swap_pairs("core")


def send(value, pairs):
    return lax.ppermute(value, AXES, pairs)


def tap_matrix(kernel, taps):
    count = kernel.shape[1]
    onehot = (taps[:, :, None] == jnp.arange(count, dtype=jnp.int32)).astype(jnp.float32)
    return jnp.einsum("ijk,uk->uij", onehot, kernel, precision=HIGHEST)


def by_h(own, other, h):
    return jnp.where(h == 0, jnp.concatenate([own, other], 0), jnp.concatenate([other, own], 0))


def body(estimate, observed, psf_taps, intersection):
    rows = intersection.shape[1] * TX
    full_width = observed.shape[2]
    depth = observed.shape[3]
    view_index = lax.axis_index("view")
    col_index = lax.axis_index("col")
    h, x = view_index // 4, view_index % 4
    column, k = col_index // 2, col_index % 2
    p = (x + column % 4) % 4
    core = k
    first_row = column * (4 * SLAB) + p * SLAB
    taps = psf_taps.shape[2]
    half = (taps - 1) // 2

    def piece(value, turn, axis):
        return lax.dynamic_slice_in_dim(value, SLAB * ((x + turn) % 2), SLAB, axis)

    def ordered(pair, first):
        one, two = pair
        return jnp.where(first, one, two), jnp.where(first, two, one)

    even = p % 2 == 0
    flipped = jnp.swapaxes(estimate, 0, 1)
    sent = [piece(flipped, turn, 1) for turn in (0, 1)]
    other, quarter = (
        jnp.concatenate(ordered([send(value, route) for value, route in zip(sent, routes)], even), 0)
        for routes in (CROSS, SPREAD)
    )
    current = by_h(quarter, other, h)
    images = [piece(observed[0], turn, 0) for turn in (0, 1)]
    *images, _ = lax.optimization_barrier((*images, quarter))
    images = [send(image, SPREAD[turn]) for turn, image in enumerate(images)]
    psf_taps, intersection, current = lax.optimization_barrier((psf_taps, intersection, current))

    kernels = psf_taps / jnp.sum(psf_taps, axis=2, keepdims=True)
    views = jnp.arange(kernels.shape[0], dtype=jnp.int32)
    own_views = 4 * h + 2 * core + jnp.stack([p % 2, (p + 1) % 2])
    picker = (own_views[:, None] == views[None, :]).astype(jnp.float32)
    own = jnp.einsum("uv,vdk->udk", picker, kernels, precision=HIGHEST)
    width = full_width // 2
    block = estimate.shape[1]
    place = jnp.arange(width, dtype=jnp.int32)
    place = place // (2 * block) * width + place % (2 * block)
    local_y = jnp.concatenate([place + core * (width // 2), place + (1 - core) * (width // 2)])
    all_y = jnp.arange(full_width, dtype=jnp.int32)
    all_z = jnp.arange(depth, dtype=jnp.int32)
    slab = jnp.arange(SLAB, dtype=jnp.int32)
    side = jnp.where(even, SLAB, -SLAB)
    wide = jnp.concatenate([slab - side, slab, slab + side])
    mat_x = tap_matrix(own[:, 0], wide[None, :] - slab[:, None] + half)
    mat_y = tap_matrix(own[:, 1], local_y[None, :] - all_y[:, None] + half)
    mat_z = tap_matrix(own[:, 2], all_z[:, None] - all_z[None, :] + half)

    wide_rows = first_row + wide
    tile = (wide_rows // TX)[:, None] == jnp.arange(intersection.shape[1], dtype=jnp.int32)[None, :]
    tile = jnp.logical_and(tile, jnp.logical_and(wide_rows >= 0, wide_rows < rows)[:, None]).astype(jnp.float32)
    masks = jnp.einsum("vt,jt->vj", intersection.astype(jnp.float32), tile, precision=HIGHEST)
    weight_rows = jnp.einsum(
        "vrj,vj->vr", tap_matrix(kernels[:, 0], slab[:, None] - wide[None, :] + half), masks, precision=HIGHEST
    )

    def coverage(kernel, places, length):
        source = places[:, None] - jnp.arange(taps, dtype=jnp.int32)[None, :] + half
        inside = jnp.logical_and(source >= 0, source < length).astype(jnp.float32)
        return jnp.einsum("yk,vk->vy", inside, kernel, precision=HIGHEST)

    weight_cols = coverage(kernels[:, 1], local_y[:width], full_width)
    weight_depth = coverage(kernels[:, 2], all_z, depth)
    weight_plane = weight_cols[:, :, None] * weight_rows[:, None, :]
    weights = jnp.einsum("vyx,vz->yxz", weight_plane, weight_depth, precision=HIGHEST)
    own_masks = jnp.einsum("uv,vj->uj", picker, masks[:, SLAB : 2 * SLAB], precision=HIGHEST)
    inside = own_masks[:, :, None, None] > 0

    scale = 1.0 / (weights + 1.0)
    for iteration in range(ITERS):
        extended = jnp.concatenate([send(current, ODD), current, send(current, EVEN)], 1)
        if iteration == 0:
            extended, scale, inside, mat_x, mat_y, mat_z, *images = lax.optimization_barrier(
                (extended, scale, inside, mat_x, mat_y, mat_z, *images)
            )
            images = lax.optimization_barrier(jnp.where(inside, jnp.stack(images), 0.0))
        extended = jnp.concatenate([extended, send(extended, SWAP_CORE)], 0)
        blurred = jnp.einsum("urj,yjz->uryz", mat_x, extended, precision=HIGH)
        blurred = jnp.einsum("urjz,uyj->uryz", blurred, mat_y, precision=HIGH)
        blurred = jnp.einsum("uryz,uzw->uryw", blurred, mat_z, precision=HIGH)
        ratio = images / jnp.where(inside, blurred, 1.0)
        back = jnp.einsum("uryw,uzw->uryz", ratio, mat_z, precision=HIGH)
        own_part, other_part = (
            jnp.einsum(
                "urj,uryz->yjz",
                mat_x,
                jnp.einsum("uryz,uyj->urjz", back, columns, precision=HIGH),
                precision=HIGH,
            )
            for columns in (mat_y[:, :, :width], mat_y[:, :, width:])
        )
        part = lax.optimization_barrier(own_part) + send(other_part, SWAP_CORE)
        part = part[:, SLAB : 2 * SLAB] + send(part[:, :SLAB], ODD) + send(part[:, 2 * SLAB :], EVEN)
        if iteration < ITERS - 1:
            current = current * (part + send(part, SWAP_H) + 1.0) * scale

    own_h = (place // width == h)[:, None, None]
    terms = current * scale * jnp.where(own_h, part + 1.0, part)
    low, high = terms[: 2 * block], terms[2 * block :]
    near = jnp.where(h == 0, low, high)
    far = jnp.where(h == 0, high, low)
    far, near = (jnp.swapaxes(value, 0, 1) for value in (far, near))
    far, near = (
        [
            send(value, reverse(route))
            for value, route in zip(ordered([half_h[:, :block], half_h[:, block:]], even), routes)
        ]
        for half_h, routes in ((far, CROSS), (near, SPREAD))
    )
    far, near = (jnp.concatenate(ordered(value, x % 2 == 0), 0) for value in (far, near))
    return near + far


def solution(mesh):
    return jax.shard_map(
        body,
        mesh=mesh,
        in_specs=(P("col", "view", None), P("view", "col", None, None), P(), P()),
        out_specs=P("col", "view", None),
        check_vma=False,
    )
```

```python
import jax
import jax.numpy as jnp
from jax import lax
from jax.sharding import PartitionSpec as P

TX = 128
ITERS = 2
HIGH = lax.Precision.HIGH
HIGHEST = lax.Precision.HIGHEST
AXES = ("view", "col")
SLAB = 16
COLS = 64


def device(h, x, c):
    return (h * 4 + x) * COLS + c


def chip_x(column, p):
    return (p - column % 4) % 4


def spread_pairs(turn):
    pairs = []
    for h in range(2):
        for column in range(COLS // 2):
            for x in range(4):
                for k in range(2):
                    p = 2 * k + (x + turn) % 2
                    pairs.append(
                        (
                            device(h, x, 2 * column + k),
                            device(h, chip_x(column, p), 2 * column + x // 2),
                        )
                    )
    return pairs


def chip_pairs(first):
    pairs = []
    for h in range(2):
        for chip in range(first, COLS // 2 * 4 - 1, 2):
            for core in range(2):
                low, high = (
                    device((h + q // 16) % 2, chip_x(q // 4, q % 4), 2 * (q // 4) + core)
                    for q in (chip, chip + 1)
                )
                pairs += [(low, high), (high, low)]
    return pairs


def swap_pairs(across):
    pairs = []
    for h in range(2):
        for x in range(4):
            for c in range(COLS):
                other = device(1 - h, x, c) if across == "h" else device(h, x, c ^ 1)
                pairs.append((device(h, x, c), other))
    return pairs


def reverse(pairs):
    return [(b, a) for a, b in pairs]


SPREAD = [spread_pairs(0), spread_pairs(1)]
ODD = chip_pairs(1)
EVEN = chip_pairs(0)
SWAP_H = swap_pairs("h")
SWAP_CORE = swap_pairs("core")


def send(value, pairs):
    return lax.ppermute(value, AXES, pairs)


def tap_matrix(kernel, taps):
    count = kernel.shape[1]
    onehot = (taps[:, :, None] == jnp.arange(count, dtype=jnp.int32)).astype(jnp.float32)
    return jnp.einsum("ijk,uk->uij", onehot, kernel, precision=HIGHEST)


def by_h(own, other, h):
    return jnp.where(h == 0, jnp.concatenate([own, other], 0), jnp.concatenate([other, own], 0))


def body(estimate, observed, psf_taps, intersection):
    rows = intersection.shape[1] * TX
    full_width = observed.shape[2]
    depth = observed.shape[3]
    view_index = lax.axis_index("view")
    col_index = lax.axis_index("col")
    h, x = view_index // 4, view_index % 4
    column, k = col_index // 2, col_index % 2
    p = (x + column % 4) % 4
    core = k
    first_row = column * (4 * SLAB) + p * SLAB
    taps = psf_taps.shape[2]
    half = (taps - 1) // 2

    def piece(value, turn, axis):
        return lax.dynamic_slice_in_dim(value, SLAB * ((x + turn) % 2), SLAB, axis)

    def ordered(pair, first):
        one, two = pair
        return jnp.where(first, one, two), jnp.where(first, two, one)

    even = p % 2 == 0
    flipped = jnp.swapaxes(estimate, 0, 1)
    quarter = jnp.concatenate(
        ordered([send(piece(flipped, turn, 1), SPREAD[turn]) for turn in (0, 1)], even), 0
    )
    current = by_h(quarter, send(quarter, SWAP_H), h)
    images = [piece(observed[0], turn, 0) for turn in (0, 1)]
    images[1], _ = lax.optimization_barrier((images[1], quarter))
    images = [send(image, SPREAD[turn]) for turn, image in enumerate(images)]
    psf_taps, intersection, current = lax.optimization_barrier((psf_taps, intersection, current))

    kernels = psf_taps / jnp.sum(psf_taps, axis=2, keepdims=True)
    views = jnp.arange(kernels.shape[0], dtype=jnp.int32)
    own_views = 4 * h + 2 * core + jnp.stack([p % 2, (p + 1) % 2])
    picker = (own_views[:, None] == views[None, :]).astype(jnp.float32)
    own = jnp.einsum("uv,vdk->udk", picker, kernels, precision=HIGHEST)
    width = full_width // 2
    block = estimate.shape[1]
    place = jnp.arange(width, dtype=jnp.int32)
    place = place // (2 * block) * width + place % (2 * block)
    local_y = jnp.concatenate([place + core * (width // 2), place + (1 - core) * (width // 2)])
    all_y = jnp.arange(full_width, dtype=jnp.int32)
    all_z = jnp.arange(depth, dtype=jnp.int32)
    slab = jnp.arange(SLAB, dtype=jnp.int32)
    side = jnp.where(even, SLAB, -SLAB)
    wide = jnp.concatenate([slab - side, slab, slab + side])
    mat_x = tap_matrix(own[:, 0], wide[None, :] - slab[:, None] + half)
    mat_y = tap_matrix(own[:, 1], local_y[None, :] - all_y[:, None] + half)
    mat_z = tap_matrix(own[:, 2], all_z[:, None] - all_z[None, :] + half)

    wide_rows = first_row + wide
    tile = (wide_rows // TX)[:, None] == jnp.arange(intersection.shape[1], dtype=jnp.int32)[None, :]
    tile = jnp.logical_and(tile, jnp.logical_and(wide_rows >= 0, wide_rows < rows)[:, None]).astype(jnp.float32)
    masks = jnp.einsum("vt,jt->vj", intersection.astype(jnp.float32), tile, precision=HIGHEST)
    weight_rows = jnp.einsum(
        "vrj,vj->vr", tap_matrix(kernels[:, 0], slab[:, None] - wide[None, :] + half), masks, precision=HIGHEST
    )

    def coverage(kernel, places, length):
        source = places[:, None] - jnp.arange(taps, dtype=jnp.int32)[None, :] + half
        inside = jnp.logical_and(source >= 0, source < length).astype(jnp.float32)
        return jnp.einsum("yk,vk->vy", inside, kernel, precision=HIGHEST)

    weight_cols = coverage(kernels[:, 1], local_y[:width], full_width)
    weight_depth = coverage(kernels[:, 2], all_z, depth)
    weight_plane = weight_cols[:, :, None] * weight_rows[:, None, :]
    weights = jnp.einsum("vyx,vz->yxz", weight_plane, weight_depth, precision=HIGHEST)
    own_masks = jnp.einsum("uv,vj->uj", picker, masks[:, SLAB : 2 * SLAB], precision=HIGHEST)
    inside = own_masks[:, :, None, None] > 0

    def with_halo(field):
        return jnp.concatenate([send(field, ODD), field, send(field, EVEN)], 1)

    scale = 1.0 / (weights + 1.0)
    extended = with_halo(current)
    for iteration in range(ITERS):
        if iteration == 0:
            extended, scale, inside, mat_x, mat_y, mat_z, *images = lax.optimization_barrier(
                (extended, scale, inside, mat_x, mat_y, mat_z, *images)
            )
            images = lax.optimization_barrier(jnp.where(inside, jnp.stack(images), 0.0))
        extended = jnp.concatenate([extended, send(extended, SWAP_CORE)], 0)
        blurred = jnp.einsum("urj,yjz->uryz", mat_x, extended, precision=HIGH)
        blurred = jnp.einsum("urjz,uyj->uryz", blurred, mat_y, precision=HIGH)
        blurred = jnp.einsum("uryz,uzw->uryw", blurred, mat_z, precision=HIGH)
        ratio = images / jnp.where(inside, blurred, 1.0)
        back = jnp.einsum("uryw,uzw->uryz", ratio, mat_z, precision=HIGH)
        own_part, other_part = (
            jnp.einsum(
                "urj,uryz->yjz",
                mat_x,
                jnp.einsum("uryz,uyj->urjz", back, columns, precision=HIGH),
                precision=HIGH,
            )
            for columns in (mat_y[:, :, :width], mat_y[:, :, width:])
        )
        part = lax.optimization_barrier(own_part) + send(other_part, SWAP_CORE)
        part = part[:, SLAB : 2 * SLAB] + send(part[:, :SLAB], ODD) + send(part[:, 2 * SLAB :], EVEN)
        if iteration < ITERS - 1:
            pieces = lax.optimization_barrier((part[: 2 * block], part[2 * block :]))
            received = [send(value, SWAP_H) for value in pieces]
            chunks = []
            for place_of, value in enumerate(pieces):
                chunk = slice(2 * block * place_of, 2 * block * (place_of + 1))
                if chunks:
                    received[1], _ = lax.optimization_barrier((received[1], chunks[0]))
                total = value + received[place_of] + 1.0
                chunks.append(current[chunk] * total * scale[chunk])
            current = jnp.concatenate(chunks, 0)
            extended = jnp.concatenate([with_halo(chunk) for chunk in chunks], 0)

    def own_half(value, mine):
        return jnp.where((h == 0) == mine, value[: 2 * block], value[2 * block :])

    total = own_half(part, True) + send(own_half(part, False), SWAP_H)
    quarter = own_half(current, True) * (total + 1.0) * own_half(scale, True)

    quarter = jnp.swapaxes(quarter, 0, 1)
    result = ordered([quarter[:, :block], quarter[:, block:]], even)
    result = lax.optimization_barrier(tuple(result))
    result = [send(value, reverse(route)) for value, route in zip(result, SPREAD)]
    return jnp.concatenate(ordered(result, x % 2 == 0), 0)


def solution(mesh):
    return jax.shard_map(
        body,
        mesh=mesh,
        in_specs=(P("col", "view", None), P("view", "col", None, None), P(), P()),
        out_specs=P("col", "view", None),
        check_vma=False,
    )
```

```python
import jax
import jax.numpy as jnp
from jax import lax
from jax.experimental.layout import Layout, with_layout_constraint
from jax.sharding import PartitionSpec as P

TX = 128
ITERS = 2
HIGH = lax.Precision.HIGH
HIGHEST = lax.Precision.HIGHEST
AXES = ("view", "col")
SLAB = 16
COLS = 64


def device(h, x, c):
    return (h * 4 + x) * COLS + c


def chip_x(column, p):
    return (p - column % 4) % 4


def spread_pairs(turn):
    pairs = []
    for h in range(2):
        for column in range(COLS // 2):
            for x in range(4):
                for k in range(2):
                    p = 2 * k + (x + turn) % 2
                    pairs.append(
                        (
                            device(h, x, 2 * column + k),
                            device(h, chip_x(column, p), 2 * column + x // 2),
                        )
                    )
    return pairs


def chip_pairs(first):
    pairs = []
    for h in range(2):
        for chip in range(first, COLS // 2 * 4 - 1, 2):
            for core in range(2):
                low, high = (
                    device((h + q // 16) % 2, chip_x(q // 4, q % 4), 2 * (q // 4) + core)
                    for q in (chip, chip + 1)
                )
                pairs += [(low, high), (high, low)]
    return pairs


def swap_pairs(across):
    pairs = []
    for h in range(2):
        for x in range(4):
            for c in range(COLS):
                other = device(1 - h, x, c) if across == "h" else device(h, x, c ^ 1)
                pairs.append((device(h, x, c), other))
    return pairs


def reverse(pairs):
    return [(b, a) for a, b in pairs]


SPREAD = [spread_pairs(0), spread_pairs(1)]
ODD = chip_pairs(1)
EVEN = chip_pairs(0)
SWAP_H = swap_pairs("h")
SWAP_CORE = swap_pairs("core")


def send(value, pairs):
    return lax.ppermute(value, AXES, pairs)


def tap_matrix(kernel, taps):
    count = kernel.shape[1]
    onehot = (taps[:, :, None] == jnp.arange(count, dtype=jnp.int32)).astype(jnp.float32)
    return jnp.einsum("ijk,uk->uij", onehot, kernel, precision=HIGHEST)


def by_h(own, other, h):
    return jnp.where(h == 0, jnp.concatenate([own, other], 0), jnp.concatenate([other, own], 0))


def body(estimate, observed, psf_taps, intersection):
    rows = intersection.shape[1] * TX
    full_width = observed.shape[2]
    depth = observed.shape[3]
    view_index = lax.axis_index("view")
    col_index = lax.axis_index("col")
    h, x = view_index // 4, view_index % 4
    column, k = col_index // 2, col_index % 2
    p = (x + column % 4) % 4
    core = k
    first_row = column * (4 * SLAB) + p * SLAB
    taps = psf_taps.shape[2]
    half = (taps - 1) // 2

    def piece(value, turn, axis):
        return lax.dynamic_slice_in_dim(value, SLAB * ((x + turn) % 2), SLAB, axis)

    def ordered(pair, first):
        one, two = pair
        return jnp.where(first, one, two), jnp.where(first, two, one)

    even = p % 2 == 0
    flipped = jnp.swapaxes(estimate, 0, 1)
    quarter = jnp.concatenate(
        ordered([send(piece(flipped, turn, 1), SPREAD[turn]) for turn in (0, 1)], even), 0
    )
    current = by_h(quarter, send(quarter, SWAP_H), h)
    images = [piece(observed[0], turn, 0) for turn in (0, 1)]
    images[1], _ = lax.optimization_barrier((images[1], quarter))
    images = [send(image, SPREAD[turn]) for turn, image in enumerate(images)]
    psf_taps, intersection, current = lax.optimization_barrier((psf_taps, intersection, current))

    kernels = psf_taps / jnp.sum(psf_taps, axis=2, keepdims=True)
    views = jnp.arange(kernels.shape[0], dtype=jnp.int32)
    own_views = 4 * h + 2 * core + jnp.stack([p % 2, (p + 1) % 2])
    picker = (own_views[:, None] == views[None, :]).astype(jnp.float32)
    own = jnp.einsum("uv,vdk->udk", picker, kernels, precision=HIGHEST)
    width = full_width // 2
    block = estimate.shape[1]
    place = jnp.arange(width, dtype=jnp.int32)
    place = place // (2 * block) * width + place % (2 * block)
    local_y = jnp.concatenate([place + core * (width // 2), place + (1 - core) * (width // 2)])
    all_y = jnp.arange(full_width, dtype=jnp.int32)
    all_z = jnp.arange(depth, dtype=jnp.int32)
    slab = jnp.arange(SLAB, dtype=jnp.int32)
    side = jnp.where(even, SLAB, -SLAB)
    wide = jnp.concatenate([slab - side, slab, slab + side])
    mat_x = tap_matrix(own[:, 0], wide[None, :] - slab[:, None] + half)
    mat_y = tap_matrix(own[:, 1], local_y[None, :] - all_y[:, None] + half)
    mat_z = tap_matrix(own[:, 2], all_z[:, None] - all_z[None, :] + half)

    mat_x, mat_y, mat_own, mat_other, mat_z = (
        with_layout_constraint(table, Layout((0, 1, 2)))
        for table in (mat_x, mat_y, mat_y[:, :, :width], mat_y[:, :, width:], mat_z)
    )

    def masks_of(intersection):
        wide_rows = first_row + wide
        tile = (wide_rows // TX)[:, None] == jnp.arange(intersection.shape[1], dtype=jnp.int32)[None, :]
        tile = jnp.logical_and(tile, jnp.logical_and(wide_rows >= 0, wide_rows < rows)[:, None])
        return jnp.einsum(
            "vt,jt->vj", intersection.astype(jnp.float32), tile.astype(jnp.float32), precision=HIGHEST
        )

    def coverage(kernel, places, length):
        source = places[:, None] - jnp.arange(taps, dtype=jnp.int32)[None, :] + half
        inside = jnp.logical_and(source >= 0, source < length).astype(jnp.float32)
        return jnp.einsum("yk,vk->vy", inside, kernel, precision=HIGHEST)

    def scale_of(psf_taps, intersection):
        kernels = psf_taps / jnp.sum(psf_taps, axis=2, keepdims=True)
        weight_rows = jnp.einsum(
            "vrj,vj->vr",
            tap_matrix(kernels[:, 0], slab[:, None] - wide[None, :] + half),
            masks_of(intersection),
            precision=HIGHEST,
        )
        weight_cols = coverage(kernels[:, 1], local_y[:width], full_width)
        weight_depth = coverage(kernels[:, 2], all_z, depth)
        weight_plane = weight_cols[:, :, None] * weight_rows[:, None, :]
        return 1.0 / (jnp.einsum("vyx,vz->yxz", weight_plane, weight_depth, precision=HIGHEST) + 1.0)

    own_masks = jnp.einsum("uv,vj->uj", picker, masks_of(intersection)[:, SLAB : 2 * SLAB], precision=HIGHEST)
    inside = own_masks[:, :, None, None] > 0

    for iteration in range(ITERS):
        extended = jnp.concatenate([send(current, ODD), current, send(current, EVEN)], 1)
        if iteration == 0:
            extended, inside, mat_x, mat_y, mat_own, mat_other, mat_z, *images = lax.optimization_barrier(
                (extended, inside, mat_x, mat_y, mat_own, mat_other, mat_z, *images)
            )
            images = lax.optimization_barrier(jnp.where(inside, jnp.stack(images), 0.0))
        extended = jnp.concatenate([extended, send(extended, SWAP_CORE)], 0)
        blurred = jnp.einsum("urj,yjz->uryz", mat_x, extended, precision=HIGH)
        blurred = jnp.einsum("urjz,uyj->uryz", blurred, mat_y, precision=HIGH)
        blurred = jnp.einsum("uryz,uzw->uryw", blurred, mat_z, precision=HIGH)
        ratio = images / jnp.where(inside, blurred, 1.0)
        back = jnp.einsum("uryw,uzw->uryz", ratio, mat_z, precision=HIGH)
        own_part, other_part = (
            jnp.einsum(
                "urj,uryz->yjz",
                mat_x,
                jnp.einsum("uryz,uyj->urjz", back, columns, precision=HIGH),
                precision=HIGH,
            )
            for columns in (mat_own, mat_other)
        )
        part = lax.optimization_barrier(own_part) + send(other_part, SWAP_CORE)
        part = part[:, SLAB : 2 * SLAB] + send(part[:, :SLAB], ODD) + send(part[:, 2 * SLAB :], EVEN)
        if iteration == 0:
            scale = scale_of(*lax.optimization_barrier((psf_taps, intersection, part))[:2])
        if iteration < ITERS - 1:
            current = current * (part + send(part, SWAP_H) + 1.0) * scale

    def own_half(value, mine):
        return jnp.where((h == 0) == mine, value[: 2 * block], value[2 * block :])

    total = own_half(part, True) + send(own_half(part, False), SWAP_H)
    quarter = own_half(current, True) * (total + 1.0) * own_half(scale, True)

    quarter = jnp.swapaxes(quarter, 0, 1)
    result = ordered([quarter[:, :block], quarter[:, block:]], even)
    result = lax.optimization_barrier(tuple(result))
    result = [send(value, reverse(route)) for value, route in zip(result, SPREAD)]
    return jnp.concatenate(ordered(result, x % 2 == 0), 0)


def solution(mesh):
    return jax.shard_map(
        body,
        mesh=mesh,
        in_specs=(P("col", "view", None), P("view", "col", None, None), P(), P()),
        out_specs=P("col", "view", None),
        check_vma=False,
    )
```

```python
import jax
import jax.numpy as jnp
from jax import lax
from jax.experimental.layout import Layout, with_layout_constraint
from jax.sharding import PartitionSpec as P

TX = 128
ITERS = 2
HIGH = lax.Precision.HIGH
HIGHEST = lax.Precision.HIGHEST
AXES = ("view", "col")
SLAB = 16
COLS = 64


def device(h, x, c):
    return (h * 4 + x) * COLS + c


def chip_x(column, p):
    return (p - column % 4) % 4


def spread_pairs(turn):
    pairs = []
    for h in range(2):
        for column in range(COLS // 2):
            for x in range(4):
                for k in range(2):
                    p = 2 * k + (x + turn) % 2
                    pairs.append(
                        (
                            device(h, x, 2 * column + k),
                            device(h, chip_x(column, p), 2 * column + x // 2),
                        )
                    )
    return pairs


def chip_pairs(first):
    pairs = []
    for h in range(2):
        for chip in range(first, COLS // 2 * 4 - 1, 2):
            for core in range(2):
                low, high = (
                    device((h + q // 16) % 2, chip_x(q // 4, q % 4), 2 * (q // 4) + core)
                    for q in (chip, chip + 1)
                )
                pairs += [(low, high), (high, low)]
    return pairs


def swap_pairs(across):
    pairs = []
    for h in range(2):
        for x in range(4):
            for c in range(COLS):
                other = device(1 - h, x, c) if across == "h" else device(h, x, c ^ 1)
                pairs.append((device(h, x, c), other))
    return pairs


def reverse(pairs):
    return [(b, a) for a, b in pairs]


SPREAD = [spread_pairs(0), spread_pairs(1)]
ODD = chip_pairs(1)
EVEN = chip_pairs(0)
SWAP_H = swap_pairs("h")
SWAP_CORE = swap_pairs("core")


def send(value, pairs):
    return lax.ppermute(value, AXES, pairs)


def tap_matrix(kernel, taps):
    count = kernel.shape[1]
    onehot = (taps[:, :, None] == jnp.arange(count, dtype=jnp.int32)).astype(jnp.float32)
    return jnp.einsum("ijk,uk->uij", onehot, kernel, precision=HIGHEST)


def by_h(own, other, h):
    return jnp.where(h == 0, jnp.concatenate([own, other], 0), jnp.concatenate([other, own], 0))


def body(estimate, observed, psf_taps, intersection):
    rows = intersection.shape[1] * TX
    full_width = observed.shape[2]
    depth = observed.shape[3]
    view_index = lax.axis_index("view")
    col_index = lax.axis_index("col")
    h, x = view_index // 4, view_index % 4
    column, k = col_index // 2, col_index % 2
    p = (x + column % 4) % 4
    core = k
    first_row = column * (4 * SLAB) + p * SLAB
    taps = psf_taps.shape[2]
    half = (taps - 1) // 2

    def piece(value, turn, axis):
        return lax.dynamic_slice_in_dim(value, SLAB * ((x + turn) % 2), SLAB, axis)

    def ordered(pair, first):
        one, two = pair
        return jnp.where(first, one, two), jnp.where(first, two, one)

    even = p % 2 == 0
    flipped = jnp.swapaxes(estimate, 0, 1)
    quarter = jnp.concatenate(
        ordered([send(piece(flipped, turn, 1), SPREAD[turn]) for turn in (0, 1)], even), 0
    )
    current = by_h(quarter, send(quarter, SWAP_H), h)
    images = [piece(observed[0], turn, 0) for turn in (0, 1)]
    *images, _ = lax.optimization_barrier((*images, quarter))
    images = [send(image, SPREAD[turn]) for turn, image in enumerate(images)]
    psf_taps, intersection, current = lax.optimization_barrier((psf_taps, intersection, current))

    kernels = psf_taps / jnp.sum(psf_taps, axis=2, keepdims=True)
    views = jnp.arange(kernels.shape[0], dtype=jnp.int32)
    own_views = 4 * h + 2 * core + jnp.stack([p % 2, (p + 1) % 2])
    picker = (own_views[:, None] == views[None, :]).astype(jnp.float32)
    own = jnp.einsum("uv,vdk->udk", picker, kernels, precision=HIGHEST)
    width = full_width // 2
    block = estimate.shape[1]
    place = jnp.arange(width, dtype=jnp.int32)
    place = place // (2 * block) * width + place % (2 * block)
    local_y = jnp.concatenate([place + core * (width // 2), place + (1 - core) * (width // 2)])
    all_y = jnp.arange(full_width, dtype=jnp.int32)
    all_z = jnp.arange(depth, dtype=jnp.int32)
    slab = jnp.arange(SLAB, dtype=jnp.int32)
    side = jnp.where(even, SLAB, -SLAB)
    wide = jnp.concatenate([slab - side, slab, slab + side])
    mat_x = tap_matrix(own[:, 0], wide[None, :] - slab[:, None] + half)
    mat_y = tap_matrix(own[:, 1], local_y[None, :] - all_y[:, None] + half)
    mat_z = tap_matrix(own[:, 2], all_z[:, None] - all_z[None, :] + half)

    mat_x, mat_y, mat_own, mat_other, mat_z = (
        with_layout_constraint(table, Layout((0, 1, 2)))
        for table in (mat_x, mat_y, mat_y[:, :, :width], mat_y[:, :, width:], mat_z)
    )

    def masks_of(intersection):
        wide_rows = first_row + wide
        tile = (wide_rows // TX)[:, None] == jnp.arange(intersection.shape[1], dtype=jnp.int32)[None, :]
        tile = jnp.logical_and(tile, jnp.logical_and(wide_rows >= 0, wide_rows < rows)[:, None])
        return jnp.einsum(
            "vt,jt->vj", intersection.astype(jnp.float32), tile.astype(jnp.float32), precision=HIGHEST
        )

    def coverage(kernel, places, length):
        source = places[:, None] - jnp.arange(taps, dtype=jnp.int32)[None, :] + half
        inside = jnp.logical_and(source >= 0, source < length).astype(jnp.float32)
        return jnp.einsum("yk,vk->vy", inside, kernel, precision=HIGHEST)

    def scale_of(psf_taps, intersection):
        kernels = psf_taps / jnp.sum(psf_taps, axis=2, keepdims=True)
        weight_rows = jnp.einsum(
            "vrj,vj->vr",
            tap_matrix(kernels[:, 0], slab[:, None] - wide[None, :] + half),
            masks_of(intersection),
            precision=HIGHEST,
        )
        weight_cols = coverage(kernels[:, 1], local_y[:width], full_width)
        weight_depth = coverage(kernels[:, 2], all_z, depth)
        weight_plane = weight_cols[:, :, None] * weight_rows[:, None, :]
        return 1.0 / (jnp.einsum("vyx,vz->yxz", weight_plane, weight_depth, precision=HIGHEST) + 1.0)

    own_masks = jnp.einsum("uv,vj->uj", picker, masks_of(intersection)[:, SLAB : 2 * SLAB], precision=HIGHEST)
    inside = own_masks[:, :, None, None] > 0

    for iteration in range(ITERS):
        extended = jnp.concatenate([send(current, ODD), current, send(current, EVEN)], 1)
        if iteration == 0:
            extended, inside, mat_x, mat_y, mat_own, mat_other, mat_z, *images = lax.optimization_barrier(
                (extended, inside, mat_x, mat_y, mat_own, mat_other, mat_z, *images)
            )
            images = lax.optimization_barrier(jnp.where(inside, jnp.stack(images), 0.0))
        extended = jnp.concatenate([extended, send(extended, SWAP_CORE)], 0)
        blurred = jnp.einsum("urj,yjz->uryz", mat_x, extended, precision=HIGH)
        blurred = jnp.einsum("urjz,uyj->uryz", blurred, mat_y, precision=HIGH)
        blurred = jnp.einsum("uryz,uzw->uryw", blurred, mat_z, precision=HIGH)
        ratio = images / jnp.where(inside, blurred, 1.0)
        back = jnp.einsum("uryw,uzw->uryz", ratio, mat_z, precision=HIGH)
        own_part, other_part = (
            jnp.einsum(
                "urj,uryz->yjz",
                mat_x,
                jnp.einsum("uryz,uyj->urjz", back, columns, precision=HIGH),
                precision=HIGH,
            )
            for columns in (mat_own, mat_other)
        )
        part = lax.optimization_barrier(own_part) + send(other_part, SWAP_CORE)
        part = part[:, SLAB : 2 * SLAB] + send(part[:, :SLAB], ODD) + send(part[:, 2 * SLAB :], EVEN)
        if iteration == 0:
            scale = scale_of(*lax.optimization_barrier((psf_taps, intersection, part))[:2])
        if iteration < ITERS - 1:
            current = current * (part + send(part, SWAP_H) + 1.0) * scale

    def own_half(value, mine):
        return jnp.where((h == 0) == mine, value[: 2 * block], value[2 * block :])

    total = own_half(part, True) + send(own_half(part, False), SWAP_H)
    quarter = own_half(current, True) * (total + 1.0) * own_half(scale, True)

    quarter = jnp.swapaxes(quarter, 0, 1)
    result = ordered([quarter[:, :block], quarter[:, block:]], even)
    result = [with_layout_constraint(value, Layout((0, 1, 2))) for value in result]
    result = [send(value, reverse(route)) for value, route in zip(result, SPREAD)]
    return jnp.concatenate(ordered(result, x % 2 == 0), 0)


def solution(mesh):
    return jax.shard_map(
        body,
        mesh=mesh,
        in_specs=(P("col", "view", None), P("view", "col", None, None), P(), P()),
        out_specs=P("col", "view", None),
        check_vma=False,
    )
```

```python
import jax
import jax.numpy as jnp
from jax import lax
from jax.experimental.layout import Layout, with_layout_constraint
from jax.sharding import PartitionSpec as P

TX = 128
ITERS = 2
HIGH = lax.Precision.HIGH
HIGHEST = lax.Precision.HIGHEST
AXES = ("view", "col")
SLAB = 16
COLS = 64


def device(h, x, c):
    return (h * 4 + x) * COLS + c


def chip_x(column, p):
    return (p - column % 4) % 4


def spread_pairs(turn):
    pairs = []
    for h in range(2):
        for column in range(COLS // 2):
            for x in range(4):
                for k in range(2):
                    p = 2 * k + (x + turn) % 2
                    pairs.append(
                        (
                            device(h, x, 2 * column + k),
                            device(h, chip_x(column, p), 2 * column + x // 2),
                        )
                    )
    return pairs


def chip_pairs(first):
    pairs = []
    for h in range(2):
        for chip in range(first, COLS // 2 * 4 - 1, 2):
            for core in range(2):
                low, high = (
                    device((h + q // 16) % 2, chip_x(q // 4, q % 4), 2 * (q // 4) + core)
                    for q in (chip, chip + 1)
                )
                pairs += [(low, high), (high, low)]
    return pairs


def swap_pairs(across):
    pairs = []
    for h in range(2):
        for x in range(4):
            for c in range(COLS):
                other = device(1 - h, x, c) if across == "h" else device(h, x, c ^ 1)
                pairs.append((device(h, x, c), other))
    return pairs


def reverse(pairs):
    return [(b, a) for a, b in pairs]


SPREAD = [spread_pairs(0), spread_pairs(1)]
ODD = chip_pairs(1)
EVEN = chip_pairs(0)
SWAP_H = swap_pairs("h")
SWAP_CORE = swap_pairs("core")


def send(value, pairs):
    return lax.ppermute(value, AXES, pairs)


def tap_matrix(kernel, taps):
    count = kernel.shape[1]
    onehot = (taps[:, :, None] == jnp.arange(count, dtype=jnp.int32)).astype(jnp.float32)
    return jnp.einsum("ijk,uk->uij", onehot, kernel, precision=HIGHEST)


def by_h(own, other, h):
    return jnp.where(h == 0, jnp.concatenate([own, other], 0), jnp.concatenate([other, own], 0))


def body(estimate, observed, psf_taps, intersection):
    rows = intersection.shape[1] * TX
    full_width = observed.shape[2]
    depth = observed.shape[3]
    view_index = lax.axis_index("view")
    col_index = lax.axis_index("col")
    h, x = view_index // 4, view_index % 4
    column, k = col_index // 2, col_index % 2
    p = (x + column % 4) % 4
    core = k
    first_row = column * (4 * SLAB) + p * SLAB
    taps = psf_taps.shape[2]
    half = (taps - 1) // 2

    def piece(value, turn, axis):
        return lax.dynamic_slice_in_dim(value, SLAB * ((x + turn) % 2), SLAB, axis)

    def ordered(pair, first):
        one, two = pair
        return jnp.where(first, one, two), jnp.where(first, two, one)

    even = p % 2 == 0
    flipped = jnp.swapaxes(estimate, 0, 1)
    quarter = jnp.concatenate(
        ordered([send(piece(flipped, turn, 1), SPREAD[turn]) for turn in (0, 1)], even), 0
    )
    current = by_h(quarter, send(quarter, SWAP_H), h)
    images = [piece(observed[0], turn, 0) for turn in (0, 1)]
    images[1], _ = lax.optimization_barrier((images[1], quarter))
    images = [send(image, SPREAD[turn]) for turn, image in enumerate(images)]
    psf_taps, intersection, current = lax.optimization_barrier((psf_taps, intersection, current))

    kernels = psf_taps / jnp.sum(psf_taps, axis=2, keepdims=True)
    views = jnp.arange(kernels.shape[0], dtype=jnp.int32)
    own_views = 4 * h + 2 * core + jnp.stack([p % 2, (p + 1) % 2])
    picker = (own_views[:, None] == views[None, :]).astype(jnp.float32)
    own = jnp.einsum("uv,vdk->udk", picker, kernels, precision=HIGHEST)
    width = full_width // 2
    block = estimate.shape[1]
    place = jnp.arange(width, dtype=jnp.int32)
    place = place // (2 * block) * width + place % (2 * block)
    local_y = jnp.concatenate([place + core * (width // 2), place + (1 - core) * (width // 2)])
    all_y = jnp.arange(full_width, dtype=jnp.int32)
    all_z = jnp.arange(depth, dtype=jnp.int32)
    slab = jnp.arange(SLAB, dtype=jnp.int32)
    side = jnp.where(even, SLAB, -SLAB)
    wide = jnp.concatenate([slab - side, slab, slab + side])
    mat_x = tap_matrix(own[:, 0], wide[None, :] - slab[:, None] + half)
    mat_y = tap_matrix(own[:, 1], local_y[None, :] - all_y[:, None] + half)
    mat_z = tap_matrix(own[:, 2], all_z[:, None] - all_z[None, :] + half)

    mat_x, mat_y, mat_own, mat_other, mat_z = (
        with_layout_constraint(table, Layout((0, 1, 2)))
        for table in (mat_x, mat_y, mat_y[:, :, :width], mat_y[:, :, width:], mat_z)
    )

    def masks_of(intersection):
        wide_rows = first_row + wide
        tile = (wide_rows // TX)[:, None] == jnp.arange(intersection.shape[1], dtype=jnp.int32)[None, :]
        tile = jnp.logical_and(tile, jnp.logical_and(wide_rows >= 0, wide_rows < rows)[:, None])
        return jnp.einsum(
            "vt,jt->vj", intersection.astype(jnp.float32), tile.astype(jnp.float32), precision=HIGHEST
        )

    def coverage(kernel, places, length):
        source = places[:, None] - jnp.arange(taps, dtype=jnp.int32)[None, :] + half
        inside = jnp.logical_and(source >= 0, source < length).astype(jnp.float32)
        return jnp.einsum("yk,vk->vy", inside, kernel, precision=HIGHEST)

    def scale_of(psf_taps, intersection):
        kernels = psf_taps / jnp.sum(psf_taps, axis=2, keepdims=True)
        weight_rows = jnp.einsum(
            "vrj,vj->vr",
            tap_matrix(kernels[:, 0], slab[:, None] - wide[None, :] + half),
            masks_of(intersection),
            precision=HIGHEST,
        )
        weight_cols = coverage(kernels[:, 1], local_y[:width], full_width)
        weight_depth = coverage(kernels[:, 2], all_z, depth)
        weight_plane = weight_cols[:, :, None] * weight_rows[:, None, :]
        return 1.0 / (jnp.einsum("vyx,vz->yxz", weight_plane, weight_depth, precision=HIGHEST) + 1.0)

    own_masks = jnp.einsum("uv,vj->uj", picker, masks_of(intersection)[:, SLAB : 2 * SLAB], precision=HIGHEST)
    inside = own_masks[:, :, None, None] > 0

    for iteration in range(ITERS):
        extended = jnp.concatenate([send(current, ODD), current, send(current, EVEN)], 1)
        if iteration == 0:
            extended, inside, mat_x, mat_y, mat_own, mat_other, mat_z, *images = lax.optimization_barrier(
                (extended, inside, mat_x, mat_y, mat_own, mat_other, mat_z, *images)
            )
            images = lax.optimization_barrier(jnp.where(inside, jnp.stack(images), 0.0))
        extended = jnp.concatenate([extended, send(extended, SWAP_CORE)], 0)
        blurred = jnp.einsum("urj,yjz->uryz", mat_x, extended, precision=HIGH)
        blurred = jnp.einsum("urjz,uyj->uryz", blurred, mat_y, precision=HIGH)
        blurred = jnp.einsum("uryz,uzw->uryw", blurred, mat_z, precision=HIGH)
        ratio = images / jnp.where(inside, blurred, 1.0)
        back = jnp.einsum("uryw,uzw->uryz", ratio, mat_z, precision=HIGH)
        own_part, other_part = (
            jnp.einsum(
                "urj,uryz->yjz",
                mat_x,
                jnp.einsum("uryz,uyj->urjz", back, columns, precision=HIGH),
                precision=HIGH,
            )
            for columns in (mat_own, mat_other)
        )
        own_part = lax.optimization_barrier(own_part)
        other_part = send(other_part, SWAP_CORE)
        to_odd, kept, to_even = (
            own_part[:, start : start + SLAB] + other_part[:, start : start + SLAB]
            for start in range(0, 3 * SLAB, SLAB)
        )
        terms = [kept, send(to_odd, ODD), send(to_even, EVEN)]
        part = sum(terms)
        if iteration == 0:
            scale = scale_of(*lax.optimization_barrier((psf_taps, intersection, part))[:2])
        if iteration < ITERS - 1:
            current = current * (part + send(part, SWAP_H) + 1.0) * scale

    def own_half(value, mine):
        return jnp.where((h == 0) == mine, value[: 2 * block], value[2 * block :])

    far, near = (sum(own_half(term, mine) for term in terms) for mine in (False, True))
    quarter = own_half(current, True) * (near + send(far, SWAP_H) + 1.0) * own_half(scale, True)

    quarter = jnp.swapaxes(quarter, 0, 1)
    result = ordered([quarter[:, :block], quarter[:, block:]], even)
    result = lax.optimization_barrier(tuple(result))
    result = [send(value, reverse(route)) for value, route in zip(result, SPREAD)]
    return jnp.concatenate(ordered(result, x % 2 == 0), 0)


def solution(mesh):
    return jax.shard_map(
        body,
        mesh=mesh,
        in_specs=(P("col", "view", None), P("view", "col", None, None), P(), P()),
        out_specs=P("col", "view", None),
        check_vma=False,
    )
```

```python
import jax
import jax.numpy as jnp
from jax import lax
from jax.experimental.layout import Layout, with_layout_constraint
from jax.sharding import PartitionSpec as P

TX = 128
ITERS = 2
HIGH = lax.Precision.HIGH
HIGHEST = lax.Precision.HIGHEST
AXES = ("view", "col")
SLAB = 16
COLS = 64


def device(h, x, c):
    return (h * 4 + x) * COLS + c


def chip_x(column, p):
    return (p - column % 4) % 4


def spread_pairs(turn):
    pairs = []
    for h in range(2):
        for column in range(COLS // 2):
            for x in range(4):
                for k in range(2):
                    p = 2 * k + (x + turn) % 2
                    pairs.append(
                        (
                            device(h, x, 2 * column + k),
                            device(h, chip_x(column, p), 2 * column + x // 2),
                        )
                    )
    return pairs


def chip_pairs(first):
    pairs = []
    for h in range(2):
        for chip in range(first, COLS // 2 * 4 - 1, 2):
            for core in range(2):
                low, high = (
                    device((h + q // 16) % 2, chip_x(q // 4, q % 4), 2 * (q // 4) + core)
                    for q in (chip, chip + 1)
                )
                pairs += [(low, high), (high, low)]
    return pairs


def swap_pairs(across):
    pairs = []
    for h in range(2):
        for x in range(4):
            for c in range(COLS):
                other = device(1 - h, x, c) if across == "h" else device(h, x, c ^ 1)
                pairs.append((device(h, x, c), other))
    return pairs


def reverse(pairs):
    return [(b, a) for a, b in pairs]


SPREAD = [spread_pairs(0), spread_pairs(1)]
ODD = chip_pairs(1)
EVEN = chip_pairs(0)
SWAP_H = swap_pairs("h")
SWAP_CORE = swap_pairs("core")


def send(value, pairs):
    return lax.ppermute(value, AXES, pairs)


def tap_matrix(kernel, taps):
    count = kernel.shape[1]
    onehot = (taps[:, :, None] == jnp.arange(count, dtype=jnp.int32)).astype(jnp.float32)
    return jnp.einsum("ijk,uk->uij", onehot, kernel, precision=HIGHEST)


def by_h(own, other, h):
    return jnp.where(h == 0, jnp.concatenate([own, other], 0), jnp.concatenate([other, own], 0))


def body(estimate, observed, psf_taps, intersection):
    rows = intersection.shape[1] * TX
    full_width = observed.shape[2]
    depth = observed.shape[3]
    view_index = lax.axis_index("view")
    col_index = lax.axis_index("col")
    h, x = view_index // 4, view_index % 4
    column, k = col_index // 2, col_index % 2
    p = (x + column % 4) % 4
    core = k
    first_row = column * (4 * SLAB) + p * SLAB
    taps = psf_taps.shape[2]
    half = (taps - 1) // 2

    def piece(value, turn, axis):
        return lax.dynamic_slice_in_dim(value, SLAB * ((x + turn) % 2), SLAB, axis)

    def joined(pair, first, axis):
        return jnp.where(first, jnp.concatenate(pair, axis), jnp.concatenate(pair[::-1], axis))

    even = p % 2 == 0
    flipped = jnp.swapaxes(estimate, 0, 1)
    quarter = joined([send(piece(flipped, turn, 1), SPREAD[turn]) for turn in (0, 1)], even, 0)
    current = by_h(quarter, send(quarter, SWAP_H), h)
    images = [piece(observed[0], turn, 0) for turn in (0, 1)]
    images[1], _ = lax.optimization_barrier((images[1], quarter))
    images = [send(image, SPREAD[turn]) for turn, image in enumerate(images)]
    psf_taps, intersection, current = lax.optimization_barrier((psf_taps, intersection, current))

    kernels = psf_taps / jnp.sum(psf_taps, axis=2, keepdims=True)
    views = jnp.arange(kernels.shape[0], dtype=jnp.int32)
    own_views = 4 * h + 2 * core + jnp.stack([p % 2, (p + 1) % 2])
    picker = (own_views[:, None] == views[None, :]).astype(jnp.float32)
    own = jnp.einsum("uv,vdk->udk", picker, kernels, precision=HIGHEST)
    width = full_width // 2
    block = estimate.shape[1]
    place = jnp.arange(width, dtype=jnp.int32)
    place = place // (2 * block) * width + place % (2 * block)
    local_y = jnp.concatenate([place + core * (width // 2), place + (1 - core) * (width // 2)])
    all_y = jnp.arange(full_width, dtype=jnp.int32)
    all_z = jnp.arange(depth, dtype=jnp.int32)
    slab = jnp.arange(SLAB, dtype=jnp.int32)
    side = jnp.where(even, SLAB, -SLAB)
    wide = jnp.concatenate([slab - side, slab, slab + side])
    mat_x = tap_matrix(own[:, 0], wide[None, :] - slab[:, None] + half)
    mat_y = tap_matrix(own[:, 1], local_y[None, :] - all_y[:, None] + half)
    mat_z = tap_matrix(own[:, 2], all_z[:, None] - all_z[None, :] + half)

    mat_x, mat_y, mat_own, mat_other, mat_z = (
        with_layout_constraint(table, Layout((0, 1, 2)))
        for table in (mat_x, mat_y, mat_y[:, :, :width], mat_y[:, :, width:], mat_z)
    )

    def masks_of(intersection):
        wide_rows = first_row + wide
        tile = (wide_rows // TX)[:, None] == jnp.arange(intersection.shape[1], dtype=jnp.int32)[None, :]
        tile = jnp.logical_and(tile, jnp.logical_and(wide_rows >= 0, wide_rows < rows)[:, None])
        return jnp.einsum(
            "vt,jt->vj", intersection.astype(jnp.float32), tile.astype(jnp.float32), precision=HIGHEST
        )

    def coverage(kernel, places, length):
        source = places[:, None] - jnp.arange(taps, dtype=jnp.int32)[None, :] + half
        inside = jnp.logical_and(source >= 0, source < length).astype(jnp.float32)
        return jnp.einsum("yk,vk->vy", inside, kernel, precision=HIGHEST)

    def scale_of(psf_taps, intersection):
        kernels = psf_taps / jnp.sum(psf_taps, axis=2, keepdims=True)
        weight_rows = jnp.einsum(
            "vrj,vj->vr",
            tap_matrix(kernels[:, 0], slab[:, None] - wide[None, :] + half),
            masks_of(intersection),
            precision=HIGHEST,
        )
        weight_cols = coverage(kernels[:, 1], local_y[:width], full_width)
        weight_depth = coverage(kernels[:, 2], all_z, depth)
        weight_plane = weight_cols[:, :, None] * weight_rows[:, None, :]
        return 1.0 / (jnp.einsum("vyx,vz->yxz", weight_plane, weight_depth, precision=HIGHEST) + 1.0)

    own_masks = jnp.einsum("uv,vj->uj", picker, masks_of(intersection)[:, SLAB : 2 * SLAB], precision=HIGHEST)
    inside = own_masks[:, :, None, None] > 0

    for iteration in range(ITERS):
        extended = jnp.concatenate([send(current, ODD), current, send(current, EVEN)], 1)
        if iteration == 0:
            extended, inside, mat_x, mat_y, mat_own, mat_other, mat_z, *images = lax.optimization_barrier(
                (extended, inside, mat_x, mat_y, mat_own, mat_other, mat_z, *images)
            )
            images = lax.optimization_barrier(jnp.where(inside, jnp.stack(images), 0.0))
        extended = jnp.concatenate([extended, send(extended, SWAP_CORE)], 0)
        blurred = jnp.einsum("urj,yjz->uryz", mat_x, extended, precision=HIGH)
        blurred = jnp.einsum("urjz,uyj->uryz", blurred, mat_y, precision=HIGH)
        blurred = jnp.einsum("uryz,uzw->uryw", blurred, mat_z, precision=HIGH)
        ratio = images / jnp.where(inside, blurred, 1.0)
        back = jnp.einsum("uryw,uzw->uryz", ratio, mat_z, precision=HIGH)
        own_part, other_part = (
            jnp.einsum(
                "urj,uryz->yjz",
                mat_x,
                jnp.einsum("uryz,uyj->urjz", back, columns, precision=HIGH),
                precision=HIGH,
            )
            for columns in (mat_own, mat_other)
        )
        own_part = lax.optimization_barrier(own_part)
        other_part = send(other_part, SWAP_CORE)
        to_odd, kept, to_even = (
            own_part[:, start : start + SLAB] + other_part[:, start : start + SLAB]
            for start in range(0, 3 * SLAB, SLAB)
        )
        terms = [kept, send(to_odd, ODD), send(to_even, EVEN)]
        part = sum(terms)
        if iteration == 0:
            scale = scale_of(*lax.optimization_barrier((psf_taps, intersection, part))[:2])
        if iteration < ITERS - 1:
            current = current * (part + send(part, SWAP_H) + 1.0) * scale

    def own_half(value, mine):
        return jnp.where((h == 0) == mine, value[: 2 * block], value[2 * block :])

    far, near = (sum(own_half(term, mine) for term in terms) for mine in (False, True))
    received = send(far, SWAP_H)

    result = []
    for first in (even, jnp.logical_not(even)):
        old, mine, other, factor = (
            jnp.where(first, value[:block], value[block:])
            for value in (own_half(current, True), near, received, own_half(scale, True))
        )
        result.append(old * (mine + other + 1.0) * factor)
    result = [send(value, reverse(route)) for value, route in zip(result, SPREAD)]
    return jnp.swapaxes(joined(result, x % 2 == 0, 1), 0, 1)


def solution(mesh):
    return jax.shard_map(
        body,
        mesh=mesh,
        in_specs=(P("col", "view", None), P("view", "col", None, None), P(), P()),
        out_specs=P("col", "view", None),
        check_vma=False,
    )
```

```python
import jax
import jax.numpy as jnp
from jax import lax
from jax.experimental.layout import Layout, with_layout_constraint
from jax.sharding import PartitionSpec as P

TX = 128
ITERS = 2
HIGH = lax.Precision.HIGH
HIGHEST = lax.Precision.HIGHEST
AXES = ("view", "col")
SLAB = 16
COLS = 64


def device(h, x, c):
    return (h * 4 + x) * COLS + c


def chip_x(column, p):
    return (p - column % 4) % 4


def spread_pairs(turn):
    pairs = []
    for h in range(2):
        for column in range(COLS // 2):
            for x in range(4):
                for k in range(2):
                    p = 2 * k + (x + turn) % 2
                    pairs.append(
                        (
                            device(h, x, 2 * column + k),
                            device(h, chip_x(column, p), 2 * column + x // 2),
                        )
                    )
    return pairs


def chip_pairs(first):
    pairs = []
    for h in range(2):
        for chip in range(first, COLS // 2 * 4 - 1, 2):
            for core in range(2):
                low, high = (
                    device((h + q // 16) % 2, chip_x(q // 4, q % 4), 2 * (q // 4) + core)
                    for q in (chip, chip + 1)
                )
                pairs += [(low, high), (high, low)]
    return pairs


def swap_pairs(across):
    pairs = []
    for h in range(2):
        for x in range(4):
            for c in range(COLS):
                other = device(1 - h, x, c) if across == "h" else device(h, x, c ^ 1)
                pairs.append((device(h, x, c), other))
    return pairs


def reverse(pairs):
    return [(b, a) for a, b in pairs]


SPREAD = [spread_pairs(0), spread_pairs(1)]
ODD = chip_pairs(1)
EVEN = chip_pairs(0)
SWAP_H = swap_pairs("h")
SWAP_CORE = swap_pairs("core")


def send(value, pairs):
    return lax.ppermute(value, AXES, pairs)


def tap_matrix(kernel, taps):
    count = kernel.shape[1]
    onehot = (taps[:, :, None] == jnp.arange(count, dtype=jnp.int32)).astype(jnp.float32)
    return jnp.einsum("ijk,uk->uij", onehot, kernel, precision=HIGHEST)


def by_h(own, other, h):
    return jnp.where(h == 0, jnp.concatenate([own, other], 0), jnp.concatenate([other, own], 0))


def body(estimate, observed, psf_taps, intersection):
    rows = intersection.shape[1] * TX
    full_width = observed.shape[2]
    depth = observed.shape[3]
    view_index = lax.axis_index("view")
    col_index = lax.axis_index("col")
    h, x = view_index // 4, view_index % 4
    column, k = col_index // 2, col_index % 2
    p = (x + column % 4) % 4
    core = k
    first_row = column * (4 * SLAB) + p * SLAB
    taps = psf_taps.shape[2]
    half = (taps - 1) // 2

    def piece(value, turn, axis):
        return lax.dynamic_slice_in_dim(value, SLAB * ((x + turn) % 2), SLAB, axis)

    def joined(pair, first, axis):
        return jnp.where(first, jnp.concatenate(pair, axis), jnp.concatenate(pair[::-1], axis))

    even = p % 2 == 0
    flipped = jnp.swapaxes(estimate, 0, 1)
    quarter = joined([send(piece(flipped, turn, 1), SPREAD[turn]) for turn in (0, 1)], even, 0)
    current = by_h(quarter, send(quarter, SWAP_H), h)
    images = [piece(observed[0], turn, 0) for turn in (0, 1)]
    images[0], _ = lax.optimization_barrier((images[0], quarter))
    images[1], _ = lax.optimization_barrier((images[1], current))
    images = [send(image, SPREAD[turn]) for turn, image in enumerate(images)]
    psf_taps, intersection, current = lax.optimization_barrier((psf_taps, intersection, current))

    kernels = psf_taps / jnp.sum(psf_taps, axis=2, keepdims=True)
    views = jnp.arange(kernels.shape[0], dtype=jnp.int32)
    own_views = 4 * h + 2 * core + jnp.stack([p % 2, (p + 1) % 2])
    picker = (own_views[:, None] == views[None, :]).astype(jnp.float32)
    own = jnp.einsum("uv,vdk->udk", picker, kernels, precision=HIGHEST)
    width = full_width // 2
    block = estimate.shape[1]
    place = jnp.arange(width, dtype=jnp.int32)
    place = place // (2 * block) * width + place % (2 * block)
    local_y = jnp.concatenate([place + core * (width // 2), place + (1 - core) * (width // 2)])
    all_y = jnp.arange(full_width, dtype=jnp.int32)
    all_z = jnp.arange(depth, dtype=jnp.int32)
    slab = jnp.arange(SLAB, dtype=jnp.int32)
    side = jnp.where(even, SLAB, -SLAB)
    wide = jnp.concatenate([slab - side, slab, slab + side])
    mat_x = tap_matrix(own[:, 0], wide[None, :] - slab[:, None] + half)
    mat_y = tap_matrix(own[:, 1], local_y[None, :] - all_y[:, None] + half)
    mat_z = tap_matrix(own[:, 2], all_z[:, None] - all_z[None, :] + half)

    mat_x, mat_y, mat_own, mat_other, mat_z = (
        with_layout_constraint(table, Layout((0, 1, 2)))
        for table in (mat_x, mat_y, mat_y[:, :, :width], mat_y[:, :, width:], mat_z)
    )

    def masks_of(intersection):
        wide_rows = first_row + wide
        tile = (wide_rows // TX)[:, None] == jnp.arange(intersection.shape[1], dtype=jnp.int32)[None, :]
        tile = jnp.logical_and(tile, jnp.logical_and(wide_rows >= 0, wide_rows < rows)[:, None])
        return jnp.einsum(
            "vt,jt->vj", intersection.astype(jnp.float32), tile.astype(jnp.float32), precision=HIGHEST
        )

    def coverage(kernel, places, length):
        source = places[:, None] - jnp.arange(taps, dtype=jnp.int32)[None, :] + half
        inside = jnp.logical_and(source >= 0, source < length).astype(jnp.float32)
        return jnp.einsum("yk,vk->vy", inside, kernel, precision=HIGHEST)

    def scale_of(psf_taps, intersection):
        kernels = psf_taps / jnp.sum(psf_taps, axis=2, keepdims=True)
        weight_rows = jnp.einsum(
            "vrj,vj->vr",
            tap_matrix(kernels[:, 0], slab[:, None] - wide[None, :] + half),
            masks_of(intersection),
            precision=HIGHEST,
        )
        weight_cols = coverage(kernels[:, 1], local_y[:width], full_width)
        weight_depth = coverage(kernels[:, 2], all_z, depth)
        weight_plane = weight_cols[:, :, None] * weight_rows[:, None, :]
        return 1.0 / (jnp.einsum("vyx,vz->yxz", weight_plane, weight_depth, precision=HIGHEST) + 1.0)

    own_masks = jnp.einsum("uv,vj->uj", picker, masks_of(intersection)[:, SLAB : 2 * SLAB], precision=HIGHEST)
    inside = own_masks[:, :, None, None] > 0

    for iteration in range(ITERS):
        extended = jnp.concatenate([send(current, ODD), current, send(current, EVEN)], 1)
        if iteration == 0:
            extended, inside, mat_x, mat_y, mat_own, mat_other, mat_z, *images = lax.optimization_barrier(
                (extended, inside, mat_x, mat_y, mat_own, mat_other, mat_z, *images)
            )
            images = lax.optimization_barrier(jnp.where(inside, jnp.stack(images), 0.0))
        extended = jnp.concatenate([extended, send(extended, SWAP_CORE)], 0)
        blurred = jnp.einsum("urj,yjz->uryz", mat_x, extended, precision=HIGH)
        blurred = jnp.einsum("urjz,uyj->uryz", blurred, mat_y, precision=HIGH)
        blurred = jnp.einsum("uryz,uzw->uryw", blurred, mat_z, precision=HIGH)
        ratio = images / jnp.where(inside, blurred, 1.0)
        back = jnp.einsum("uryw,uzw->uryz", ratio, mat_z, precision=HIGH)
        own_part, other_part = (
            jnp.einsum(
                "urj,uryz->yjz",
                mat_x,
                jnp.einsum("uryz,uyj->urjz", back, columns, precision=HIGH),
                precision=HIGH,
            )
            for columns in (mat_own, mat_other)
        )
        own_part = lax.optimization_barrier(own_part)
        other_part = send(other_part, SWAP_CORE)
        to_odd, kept, to_even = (
            own_part[:, start : start + SLAB] + other_part[:, start : start + SLAB]
            for start in range(0, 3 * SLAB, SLAB)
        )
        terms = [kept, send(to_odd, ODD), send(to_even, EVEN)]
        part = sum(terms)
        if iteration == 0:
            scale = scale_of(*lax.optimization_barrier((psf_taps, intersection, part))[:2])
        if iteration < ITERS - 1:
            current = current * (part + send(part, SWAP_H) + 1.0) * scale

    def own_half(value, mine):
        return jnp.where((h == 0) == mine, value[: 2 * block], value[2 * block :])

    far, near = (sum(own_half(term, mine) for term in terms) for mine in (False, True))
    received = send(far, SWAP_H)

    result = []
    for first in (even, jnp.logical_not(even)):
        old, mine, other, factor = (
            jnp.where(first, value[:block], value[block:])
            for value in (own_half(current, True), near, received, own_half(scale, True))
        )
        result.append(old * (mine + other + 1.0) * factor)
    result = [send(value, reverse(route)) for value, route in zip(result, SPREAD)]
    return jnp.swapaxes(joined(result, x % 2 == 0, 1), 0, 1)


def solution(mesh):
    return jax.shard_map(
        body,
        mesh=mesh,
        in_specs=(P("col", "view", None), P("view", "col", None, None), P(), P()),
        out_specs=P("col", "view", None),
        check_vma=False,
    )
```

```python
import jax
import jax.numpy as jnp
from jax import lax
from jax.experimental.layout import Layout, with_layout_constraint
from jax.sharding import PartitionSpec as P

TX = 128
ITERS = 2
HIGH = lax.Precision.HIGH
HIGHEST = lax.Precision.HIGHEST
AXES = ("view", "col")
SLAB = 16
COLS = 64


def device(h, x, c):
    return (h * 4 + x) * COLS + c


def chip_x(column, p):
    return (p - column % 4) % 4


def spread_pairs(turn):
    pairs = []
    for h in range(2):
        for column in range(COLS // 2):
            for x in range(4):
                for k in range(2):
                    p = 2 * k + (x + turn) % 2
                    pairs.append(
                        (
                            device(h, x, 2 * column + k),
                            device(h, chip_x(column, p), 2 * column + x // 2),
                        )
                    )
    return pairs


def chip_pairs(first):
    pairs = []
    for h in range(2):
        for chip in range(first, COLS // 2 * 4 - 1, 2):
            for core in range(2):
                low, high = (
                    device((h + q // 16) % 2, chip_x(q // 4, q % 4), 2 * (q // 4) + core)
                    for q in (chip, chip + 1)
                )
                pairs += [(low, high), (high, low)]
    return pairs


def swap_pairs(across):
    pairs = []
    for h in range(2):
        for x in range(4):
            for c in range(COLS):
                other = device(1 - h, x, c) if across == "h" else device(h, x, c ^ 1)
                pairs.append((device(h, x, c), other))
    return pairs


def reverse(pairs):
    return [(b, a) for a, b in pairs]


SPREAD = [spread_pairs(0), spread_pairs(1)]
ODD = chip_pairs(1)
EVEN = chip_pairs(0)
SWAP_H = swap_pairs("h")
SWAP_CORE = swap_pairs("core")


def send(value, pairs):
    return lax.ppermute(value, AXES, pairs)


def tap_matrix(kernel, taps):
    count = kernel.shape[1]
    onehot = (taps[:, :, None] == jnp.arange(count, dtype=jnp.int32)).astype(jnp.float32)
    return jnp.einsum("ijk,uk->uij", onehot, kernel, precision=HIGHEST)


def by_h(own, other, h):
    return jnp.where(h == 0, jnp.concatenate([own, other], 0), jnp.concatenate([other, own], 0))


def body(estimate, observed, psf_taps, intersection):
    rows = intersection.shape[1] * TX
    full_width = observed.shape[2]
    depth = observed.shape[3]
    view_index = lax.axis_index("view")
    col_index = lax.axis_index("col")
    h, x = view_index // 4, view_index % 4
    column, k = col_index // 2, col_index % 2
    p = (x + column % 4) % 4
    core = k
    first_row = column * (4 * SLAB) + p * SLAB
    taps = psf_taps.shape[2]
    half = (taps - 1) // 2

    def piece(value, turn, axis):
        return lax.dynamic_slice_in_dim(value, SLAB * ((x + turn) % 2), SLAB, axis)

    def joined(pair, first, axis):
        return jnp.where(first, jnp.concatenate(pair, axis), jnp.concatenate(pair[::-1], axis))

    even = p % 2 == 0
    flipped = jnp.swapaxes(estimate, 0, 1)
    quarter = joined([send(piece(flipped, turn, 1), SPREAD[turn]) for turn in (0, 1)], even, 0)
    current = by_h(quarter, send(quarter, SWAP_H), h)
    images = [piece(observed[0], turn, 0) for turn in (0, 1)]
    images[1], _ = lax.optimization_barrier((images[1], quarter))
    images = [send(image, SPREAD[turn]) for turn, image in enumerate(images)]
    psf_taps, intersection, current = lax.optimization_barrier((psf_taps, intersection, current))

    kernels = psf_taps / jnp.sum(psf_taps, axis=2, keepdims=True)
    views = jnp.arange(kernels.shape[0], dtype=jnp.int32)
    own_views = 4 * h + 2 * core + jnp.stack([p % 2, (p + 1) % 2])
    picker = (own_views[:, None] == views[None, :]).astype(jnp.float32)
    own = jnp.einsum("uv,vdk->udk", picker, kernels, precision=HIGHEST)
    width = full_width // 2
    block = estimate.shape[1]
    place = jnp.arange(width, dtype=jnp.int32)
    place = place // (2 * block) * width + place % (2 * block)
    local_y = jnp.concatenate([place + core * (width // 2), place + (1 - core) * (width // 2)])
    all_y = jnp.arange(full_width, dtype=jnp.int32)
    all_z = jnp.arange(depth, dtype=jnp.int32)
    slab = jnp.arange(SLAB, dtype=jnp.int32)
    side = jnp.where(even, SLAB, -SLAB)
    wide = jnp.concatenate([slab - side, slab, slab + side])
    mat_x = tap_matrix(own[:, 0], wide[None, :] - slab[:, None] + half)
    mat_y = tap_matrix(own[:, 1], local_y[None, :] - all_y[:, None] + half)
    mat_z = tap_matrix(own[:, 2], all_z[:, None] - all_z[None, :] + half)

    mat_x, mat_y, mat_own, mat_other, mat_z = (
        with_layout_constraint(table, Layout((0, 1, 2)))
        for table in (mat_x, mat_y, mat_y[:, :, :width], mat_y[:, :, width:], mat_z)
    )

    def masks_of(intersection):
        wide_rows = first_row + wide
        tile = (wide_rows // TX)[:, None] == jnp.arange(intersection.shape[1], dtype=jnp.int32)[None, :]
        tile = jnp.logical_and(tile, jnp.logical_and(wide_rows >= 0, wide_rows < rows)[:, None])
        return jnp.einsum(
            "vt,jt->vj", intersection.astype(jnp.float32), tile.astype(jnp.float32), precision=HIGHEST
        )

    def coverage(kernel, places, length):
        source = places[:, None] - jnp.arange(taps, dtype=jnp.int32)[None, :] + half
        inside = jnp.logical_and(source >= 0, source < length).astype(jnp.float32)
        return jnp.einsum("yk,vk->vy", inside, kernel, precision=HIGHEST)

    def scale_of(psf_taps, intersection):
        kernels = psf_taps / jnp.sum(psf_taps, axis=2, keepdims=True)
        weight_rows = jnp.einsum(
            "vrj,vj->vr",
            tap_matrix(kernels[:, 0], slab[:, None] - wide[None, :] + half),
            masks_of(intersection),
            precision=HIGHEST,
        )
        weight_cols = coverage(kernels[:, 1], local_y[:width], full_width)
        weight_depth = coverage(kernels[:, 2], all_z, depth)
        weight_plane = weight_cols[:, :, None] * weight_rows[:, None, :]
        return 1.0 / (jnp.einsum("vyx,vz->yxz", weight_plane, weight_depth, precision=HIGHEST) + 1.0)

    own_masks = jnp.einsum("uv,vj->uj", picker, masks_of(intersection)[:, SLAB : 2 * SLAB], precision=HIGHEST)
    inside = own_masks[:, :, None, None] > 0

    for iteration in range(ITERS):
        extended = jnp.concatenate([send(current, ODD), current, send(current, EVEN)], 1)
        if iteration == 0:
            extended, inside, mat_x, mat_y, mat_own, mat_other, mat_z, *images = lax.optimization_barrier(
                (extended, inside, mat_x, mat_y, mat_own, mat_other, mat_z, *images)
            )
            images = lax.optimization_barrier(jnp.where(inside, jnp.stack(images), 0.0))
        extended = jnp.concatenate([extended, send(extended, SWAP_CORE)], 0)
        blurred = jnp.einsum("urj,yjz->uryz", mat_x, extended, precision=HIGH)
        blurred = jnp.einsum("urjz,uyj->uryz", blurred, mat_y, precision=HIGH)
        blurred = jnp.einsum("uryz,uzw->uryw", blurred, mat_z, precision=HIGH)
        ratio = images / jnp.where(inside, blurred, 1.0)
        back = jnp.einsum("uryw,uzw->uryz", ratio, mat_z, precision=HIGH)
        own_part, other_part = (
            jnp.einsum(
                "urj,uryz->yjz",
                mat_x,
                jnp.einsum("uryz,uyj->urjz", back, columns, precision=HIGH),
                precision=HIGH,
            )
            for columns in (mat_own, mat_other)
        )
        own_part = lax.optimization_barrier(own_part)
        other_part = send(other_part, SWAP_CORE)
        to_odd, kept, to_even = (
            own_part[:, start : start + SLAB] + other_part[:, start : start + SLAB]
            for start in range(0, 3 * SLAB, SLAB)
        )
        terms = [kept, send(to_even, EVEN), send(to_odd, ODD)]
        part = sum(terms)
        if iteration == 0:
            scale = scale_of(*lax.optimization_barrier((psf_taps, intersection, part))[:2])
        if iteration < ITERS - 1:
            current = current * (part + send(part, SWAP_H) + 1.0) * scale

    def own_half(value, mine):
        return jnp.where((h == 0) == mine, value[: 2 * block], value[2 * block :])

    far, near = (sum(own_half(term, mine) for term in terms) for mine in (False, True))
    received = send(far, SWAP_H)

    result = []
    for first in (even, jnp.logical_not(even)):
        old, mine, other, factor = (
            jnp.where(first, value[:block], value[block:])
            for value in (own_half(current, True), near, received, own_half(scale, True))
        )
        result.append(old * (mine + other + 1.0) * factor)
    result = [send(value, reverse(route)) for value, route in zip(result, SPREAD)]
    return jnp.swapaxes(joined(result, x % 2 == 0, 1), 0, 1)


def solution(mesh):
    return jax.shard_map(
        body,
        mesh=mesh,
        in_specs=(P("col", "view", None), P("view", "col", None, None), P(), P()),
        out_specs=P("col", "view", None),
        check_vma=False,
    )
```
